256 devices in a mesh: section: 16 (over y_hi, z), blk: 16 (over y_lo, x, core).
Axes of the slice: x: 4, y: 4 (y_hi: 2, y_lo: 2; y = y_hi * 2 + y_lo), z: 8, core: 2. Of those that a mesh axis runs over, the one named last changes fastest.
Arguments:
- pending_groups: bfloat16 [1024, 65536], P('section', 'blk'), may hold values from -6 to 6
- coefficient_tiles: bfloat16 [16, 512, 8, 128, 128], P('section', 'blk'), may hold values from -0.25 to 0.25
- source_block_indices: int32 [16, 512, 8], P('section', 'blk'), may hold values from 0 to 511, as said below
- additive_offsets: float32 [16, 65536], P('section', 'blk'), may hold values from -1.75 to 1.75
Outputs:
- emitted: bfloat16 [8, 1024, 65536], P(None, 'section', 'blk')
The draws below stay inside these ranges and needn't reach their ends.
Inputs may be any that keep to these rules, and one draw needn't show every extreme that they name: `source_block_indices`: within a block-row the 8 block columns are distinct. A block-row held by index d of blk (block-rows d*32 to (d+1)*32 - 1) uses only block columns d*32 - 4 to (d+1)*32 + 3, taken modulo 512; in every layer the first block-row of each index uses column d*32 - 4 and the last uses (d+1)*32 + 3.
All inputs are finite; a program needn't handle non-finite values.
Results may differ from the reference program's by a relative error of at most 0.013.
Values may be sent and summed in bfloat16 or wider, within the bound.
A program may use at most 64 MiB of HBM per device.

```python
import jax
import jax.numpy as jnp
from jax import lax

BLK = 128
BR_DEV = 32
NZB = 8
HALO = 4
GROUP_HEIGHT = 64
TICKS = 8
DEPTH_OF_NET = 16
NB = 512
UNITS_PER_LEVEL = 65536


def draw_source_block_indices(key, part):
    window = BR_DEV + 2 * HALO
    scores = jax.random.randint(key, (DEPTH_OF_NET, NB, window), 0, 1 << 20)
    offsets = jnp.arange(window, dtype=jnp.int32)
    local_row = jnp.arange(NB, dtype=jnp.int32) % BR_DEV
    ranked = scores * window + offsets[None, None, :]
    first_edge = (local_row[:, None] == 0) & (offsets[None, :] == 0)
    last_edge = (local_row[:, None] == BR_DEV - 1) & (offsets[None, :] == window - 1)
    ranked = jnp.where((first_edge | last_edge)[None, :, :], -1, ranked)
    chosen = jnp.argsort(ranked, axis=-1)[:, :, :NZB].astype(jnp.int32)
    owner_start = jnp.arange(NB, dtype=jnp.int32) // BR_DEV * BR_DEV
    return jnp.mod(owner_start[None, :, None] - HALO + chosen, NB).astype(jnp.int32)


def level_of(stream_key, shape, cuts, least, top_value):
    factor_of, own = 1.0, jax.random.fold_in(stream_key, 6)
    for dim, blocks in cuts:
        steps = jnp.exp(jax.random.uniform(jax.random.fold_in(own, dim), (blocks,), jnp.float32, least / len(cuts), top_value / len(cuts)))
        factor_of = factor_of * jnp.repeat(steps, shape[dim] // blocks).reshape([-1 if axis == dim else 1 for axis in range(len(shape))])
    return factor_of


def centred(key, extent, spread, reach, shards=(), held_as=jnp.bfloat16):
    array = jax.random.normal(key, extent, jnp.float32) * spread
    if len(shards) > 0:
        array = level_of(key, extent, shards, -0.22, 0.18) * array
    return jnp.clip(array, min=-reach, max=reach).astype(held_as)


def setup_inputs(seed: int = 0) -> dict:
    splits = jax.random.split(jax.random.key(seed), 5)
    return {
        "pending_groups": centred(splits[0], (DEPTH_OF_NET * GROUP_HEIGHT, UNITS_PER_LEVEL), 1.0, 6.0, ((0, 16), (1, 16))),
        "coefficient_tiles": centred(splits[1], (DEPTH_OF_NET, NB, NZB, BLK, BLK), (NZB * BLK // 2) ** -0.5, 0.25, ((0, 16), (1, 16))),
        "source_block_indices": draw_source_block_indices(jax.random.fold_in(splits[4], 71), 0),
        "additive_offsets": centred(splits[3], (DEPTH_OF_NET, UNITS_PER_LEVEL), 0.3, 1.75, ((0, 16), (1, 16)), jnp.float32),
    }


def layer_apply(forwarded_activations, layer_weights, layer_cols, layer_bias):
    row_count = forwarded_activations.shape[0]
    blocks = forwarded_activations.reshape(row_count, NB, BLK).astype(jnp.float32)
    picked = blocks[:, layer_cols]
    summed = jnp.einsum("mikc,ikcd->mid", picked, layer_weights.astype(jnp.float32))
    summed = summed.reshape(row_count, NB * BLK) + layer_bias
    return jnp.maximum(summed, 0.0)


def one_layer(operands):
    return layer_apply(operands[0], operands[1], operands[2], operands[3])


def reference(pending_groups, coefficient_tiles, source_block_indices, additive_offsets):
    forwarded_activations = pending_groups.reshape(DEPTH_OF_NET, GROUP_HEIGHT, UNITS_PER_LEVEL)
    emitted = []
    for tick_index in range(TICKS):
        produced = lax.map(one_layer, (forwarded_activations, coefficient_tiles, source_block_indices, additive_offsets))
        live_mask = (jnp.arange(DEPTH_OF_NET) >= tick_index)[:, None, None]
        produced = jnp.where(live_mask, produced, 0.0).astype(jnp.bfloat16)
        emitted.append(produced.reshape(DEPTH_OF_NET * GROUP_HEIGHT, UNITS_PER_LEVEL))
        forwarded_activations = jnp.concatenate([jnp.zeros((1, GROUP_HEIGHT, UNITS_PER_LEVEL), jnp.bfloat16), produced[:-1]], axis=0)
    return jnp.stack(emitted)
```

```python
import functools

import jax
import jax.numpy as jnp
from jax import lax
from jax.experimental import pallas as pl
from jax.experimental.pallas import tpu as pltpu
from jax.sharding import PartitionSpec as P

BLK = 128
HALO = 4
TICKS = 8
MESH = pl.DeviceIdType.MESH


def relay_kernel(n_sec, n_blk, cols_ref, pend_ref, w_ref, b_ref, out_ref,
                 slots, work, send_sem, recv_sem, local_sem):
    s = lax.axis_index("section")
    d = lax.axis_index("blk")
    nb = pend_ref.shape[0]
    npad = nb + 2 * HALO
    left = lax.rem(d + n_blk - 1, n_blk)
    right = lax.rem(d + 1, n_blk)
    s_next = jnp.minimum(s + 1, n_sec - 1)
    s_prev = jnp.maximum(s - 1, 0)

    barrier = pltpu.get_barrier_semaphore()
    for nd in (left, right):
        pl.semaphore_signal(barrier, inc=1, device_id=(s, nd), device_id_type=MESH)

    @pl.when(s < n_sec - 1)
    def _():
        for nd in (left, d, right):
            pl.semaphore_signal(barrier, inc=1, device_id=(s_next, nd), device_id_type=MESH)

    @pl.when(s > 0)
    def _():
        for nd in (left, d, right):
            pl.semaphore_signal(barrier, inc=1, device_id=(s_prev, nd), device_id_type=MESH)

    has_prev = (s + n_sec - 1) // n_sec
    has_next = (2 * n_sec - 3 - s) // (n_sec - 1)
    pl.semaphore_wait(barrier, 2 + 3 * has_prev + 3 * has_next)

    def edge_copies(src, t, tgt_sec):
        lo = pltpu.make_async_remote_copy(
            src_ref=src.at[pl.ds(0, HALO)],
            dst_ref=slots.at[t, pl.ds(HALO + nb, HALO)],
            send_sem=send_sem.at[t, 1], recv_sem=recv_sem.at[t, 1],
            device_id=(tgt_sec, left), device_id_type=MESH)
        hi = pltpu.make_async_remote_copy(
            src_ref=src.at[pl.ds(nb - HALO, HALO)],
            dst_ref=slots.at[t, pl.ds(0, HALO)],
            send_sem=send_sem.at[t, 2], recv_sem=recv_sem.at[t, 2],
            device_id=(tgt_sec, right), device_id_type=MESH)
        return lo, hi

    def center_copy(src, t, tgt_sec):
        return pltpu.make_async_remote_copy(
            src_ref=src,
            dst_ref=slots.at[t, pl.ds(HALO, nb)],
            send_sem=send_sem.at[t, 0], recv_sem=recv_sem.at[t, 0],
            device_id=(tgt_sec, d), device_id_type=MESH)

    lo0, hi0 = edge_copies(pend_ref, 0, s)
    lo0.start()
    hi0.start()
    own = pltpu.make_async_copy(pend_ref, work.at[pl.ds(HALO, nb)], local_sem.at[0])
    own.start()
    own.wait()
    lo0.wait_recv()
    hi0.wait_recv()
    cp_lo = pltpu.make_async_copy(slots.at[0, pl.ds(0, HALO)], work.at[pl.ds(0, HALO)], local_sem.at[1])
    cp_hi = pltpu.make_async_copy(slots.at[0, pl.ds(HALO + nb, HALO)], work.at[pl.ds(HALO + nb, HALO)],
                                  local_sem.at[2])
    cp_lo.start()
    cp_hi.start()
    cp_lo.wait()
    cp_hi.wait()

    def compute(t):
        def row_body(i, carry):
            xs = [work[cols_ref[i, k]] for k in range(w_ref.shape[1] // BLK)]
            xcat = jnp.concatenate(xs, axis=1)
            acc = jnp.dot(xcat, w_ref[i], preferred_element_type=jnp.float32)
            acc = acc + b_ref[i]
            out_ref[t, i] = jnp.maximum(acc, 0.0).astype(out_ref.dtype)
            return carry
        lax.fori_loop(0, nb, row_body, 0)

    for t in range(TICKS):
        if t > 0:
            @pl.when(s >= t)
            def _():
                c = center_copy(out_ref.at[t - 1], t, s)
                lo, hi = edge_copies(out_ref.at[t - 1], t, s)
                c.wait_recv()
                lo.wait_recv()
                hi.wait_recv()
                cw = pltpu.make_async_copy(slots.at[t], work, local_sem.at[0])
                cw.start()
                cw.wait()

        @pl.when(s >= t)
        def _():
            compute(t)

        @pl.when(s < t)
        def _():
            out_ref[t] = jnp.zeros(out_ref.shape[1:], out_ref.dtype)

        if t + 1 < TICKS:
            @pl.when((s >= t) & (s < n_sec - 1))
            def _():
                c = center_copy(out_ref.at[t], t + 1, s_next)
                lo, hi = edge_copies(out_ref.at[t], t + 1, s_next)
                c.start()
                lo.start()
                hi.start()

    lo0.wait_send()
    hi0.wait_send()
    for t in range(TICKS - 1):
        @pl.when((s >= t) & (s < n_sec - 1))
        def _():
            c = center_copy(out_ref.at[t], t + 1, s_next)
            lo, hi = edge_copies(out_ref.at[t], t + 1, s_next)
            c.wait_send()
            lo.wait_send()
            hi.wait_send()


def shards(n_sec, n_blk, pending_groups, coefficient_tiles, source_block_indices, additive_offsets):
    rows, units = pending_groups.shape
    nb = coefficient_tiles.shape[1]
    nz = coefficient_tiles.shape[2]
    d = lax.axis_index("blk")
    cols = jnp.mod(source_block_indices[0] - d * nb + HALO, nb * n_blk).astype(jnp.int32)
    pend = pending_groups.reshape(rows, nb, BLK).transpose(1, 0, 2)
    w = coefficient_tiles[0].reshape(nb, nz * BLK, BLK)
    bias = additive_offsets[0].reshape(nb, 1, BLK)
    npad = nb + 2 * HALO
    out = pl.pallas_call(
        functools.partial(relay_kernel, n_sec, n_blk),
        out_shape=jax.ShapeDtypeStruct((TICKS, nb, rows, BLK), jnp.bfloat16),
        in_specs=[
            pl.BlockSpec(memory_space=pltpu.SMEM),
            pl.BlockSpec(memory_space=pltpu.VMEM),
            pl.BlockSpec(memory_space=pltpu.VMEM),
            pl.BlockSpec(memory_space=pltpu.VMEM),
        ],
        out_specs=pl.BlockSpec(memory_space=pltpu.VMEM),
        scratch_shapes=[
            pltpu.VMEM((TICKS, npad, rows, BLK), jnp.bfloat16),
            pltpu.VMEM((npad, rows, BLK), jnp.bfloat16),
            pltpu.SemaphoreType.DMA((TICKS, 3)),
            pltpu.SemaphoreType.DMA((TICKS, 3)),
            pltpu.SemaphoreType.DMA((3,)),
        ],
        compiler_params=pltpu.CompilerParams(
            collective_id=0, has_side_effects=True, vmem_limit_bytes=48 * 1024 * 1024),
    )(cols, pend, w, bias)
    return out.transpose(0, 2, 1, 3).reshape(TICKS, rows, nb * BLK)


def solution(mesh):
    n_sec = mesh.shape["section"]
    n_blk = mesh.shape["blk"]
    in_specs = (
        P("section", "blk"),
        P("section", "blk", None, None, None),
        P("section", "blk", None),
        P("section", "blk"),
    )
    out_specs = P(None, "section", "blk")
    return jax.shard_map(functools.partial(shards, n_sec, n_blk), mesh=mesh, in_specs=in_specs,
                         out_specs=out_specs, check_vma=False)
```

```python
import functools

import jax
import jax.numpy as jnp
from jax import lax
from jax.experimental import pallas as pl
from jax.experimental.pallas import tpu as pltpu
from jax.sharding import PartitionSpec as P

BLK = 128
HALO = 4
TICKS = 8
ROW_CHUNKS = 2
MESH = pl.DeviceIdType.MESH


def relay_kernel(n_sec, n_blk, n_chunk, cols_ref, pend_ref, w_ref, b_ref, out_ref,
                 slots, send_sem, recv_sem, local_sem, *works):
    s = lax.axis_index("section")
    d = lax.axis_index("blk")
    nb = pend_ref.shape[0]
    rc = pend_ref.shape[1] // n_chunk
    left = lax.rem(d + n_blk - 1, n_blk)
    right = lax.rem(d + 1, n_blk)
    s_next = jnp.minimum(s + 1, n_sec - 1)
    s_prev = jnp.maximum(s - 1, 0)

    barrier = pltpu.get_barrier_semaphore()
    for nd in (left, right):
        pl.semaphore_signal(barrier, inc=1, device_id=(s, nd), device_id_type=MESH)

    @pl.when(s < n_sec - 1)
    def _():
        for nd in (left, d, right):
            pl.semaphore_signal(barrier, inc=1, device_id=(s_next, nd), device_id_type=MESH)

    @pl.when(s > 0)
    def _():
        for nd in (left, d, right):
            pl.semaphore_signal(barrier, inc=1, device_id=(s_prev, nd), device_id_type=MESH)

    has_prev = (s + n_sec - 1) // n_sec
    has_next = (2 * n_sec - 3 - s) // (n_sec - 1)
    pl.semaphore_wait(barrier, 2 + 3 * has_prev + 3 * has_next)

    def copies(src, t, c, tgt_sec):
        rows = pl.ds(c * rc, rc)
        center = pltpu.make_async_remote_copy(
            src_ref=src.at[:, rows],
            dst_ref=slots.at[t, pl.ds(HALO, nb), rows],
            send_sem=send_sem.at[t, c, 0], recv_sem=recv_sem.at[t, c, 0],
            device_id=(tgt_sec, d), device_id_type=MESH)
        lo = pltpu.make_async_remote_copy(
            src_ref=src.at[pl.ds(0, HALO), rows],
            dst_ref=slots.at[t, pl.ds(HALO + nb, HALO), rows],
            send_sem=send_sem.at[t, c, 1], recv_sem=recv_sem.at[t, c, 1],
            device_id=(tgt_sec, left), device_id_type=MESH)
        hi = pltpu.make_async_remote_copy(
            src_ref=src.at[pl.ds(nb - HALO, HALO), rows],
            dst_ref=slots.at[t, pl.ds(0, HALO), rows],
            send_sem=send_sem.at[t, c, 2], recv_sem=recv_sem.at[t, c, 2],
            device_id=(tgt_sec, right), device_id_type=MESH)
        return center, lo, hi

    first = [copies(pend_ref, 0, c, s)[1:] for c in range(n_chunk)]
    for pair in first:
        for cp in pair:
            cp.start()
    for c in range(n_chunk):
        rows = pl.ds(c * rc, rc)
        own = pltpu.make_async_copy(pend_ref.at[:, rows], works[c].at[pl.ds(HALO, nb)], local_sem.at[0])
        own.start()
        own.wait()
        for cp in first[c]:
            cp.wait_recv()
        cp_lo = pltpu.make_async_copy(slots.at[0, pl.ds(0, HALO), rows], works[c].at[pl.ds(0, HALO)],
                                      local_sem.at[1])
        cp_hi = pltpu.make_async_copy(slots.at[0, pl.ds(HALO + nb, HALO), rows],
                                      works[c].at[pl.ds(HALO + nb, HALO)], local_sem.at[2])
        cp_lo.start()
        cp_hi.start()
        cp_lo.wait()
        cp_hi.wait()

    def compute(t, c):
        work = works[c]

        def row_body(i, carry):
            xs = [work[cols_ref[i, k]] for k in range(w_ref.shape[1] // BLK)]
            xcat = jnp.concatenate(xs, axis=1)
            acc = jnp.dot(xcat, w_ref[i], preferred_element_type=jnp.float32)
            acc = acc + b_ref[i]
            out_ref[t, i, pl.ds(c * rc, rc)] = jnp.maximum(acc, 0.0).astype(out_ref.dtype)
            return carry
        lax.fori_loop(0, nb, row_body, 0)

    for t in range(TICKS):
        for c in range(n_chunk):
            if t > 0:
                @pl.when(s >= t)
                def _():
                    for cp in copies(out_ref.at[t - 1], t, c, s):
                        cp.wait_recv()
                    cw = pltpu.make_async_copy(slots.at[t, :, pl.ds(c * rc, rc)], works[c], local_sem.at[0])
                    cw.start()
                    cw.wait()

            @pl.when(s >= t)
            def _():
                compute(t, c)

            @pl.when(s < t)
            def _():
                out_ref[t, :, pl.ds(c * rc, rc)] = jnp.zeros((nb, rc, BLK), out_ref.dtype)

            if t + 1 < TICKS:
                @pl.when((s >= t) & (s < n_sec - 1))
                def _():
                    for cp in copies(out_ref.at[t], t + 1, c, s_next):
                        cp.start()

    for pair in first:
        for cp in pair:
            cp.wait_send()
    for t in range(TICKS - 1):
        @pl.when((s >= t) & (s < n_sec - 1))
        def _():
            for c in range(n_chunk):
                for cp in copies(out_ref.at[t], t + 1, c, s_next):
                    cp.wait_send()


def shards(n_sec, n_blk, n_chunk, pending_groups, coefficient_tiles, source_block_indices, additive_offsets):
    rows, units = pending_groups.shape
    nb = coefficient_tiles.shape[1]
    nz = coefficient_tiles.shape[2]
    d = lax.axis_index("blk")
    cols = jnp.mod(source_block_indices[0] - d * nb + HALO, nb * n_blk).astype(jnp.int32)
    pend = pending_groups.reshape(rows, nb, BLK).transpose(1, 0, 2)
    w = coefficient_tiles[0].reshape(nb, nz * BLK, BLK)
    bias = additive_offsets[0].reshape(nb, 1, BLK)
    npad = nb + 2 * HALO
    out = pl.pallas_call(
        functools.partial(relay_kernel, n_sec, n_blk, n_chunk),
        out_shape=jax.ShapeDtypeStruct((TICKS, nb, rows, BLK), jnp.bfloat16),
        in_specs=[
            pl.BlockSpec(memory_space=pltpu.SMEM),
            pl.BlockSpec(memory_space=pltpu.VMEM),
            pl.BlockSpec(memory_space=pltpu.VMEM),
            pl.BlockSpec(memory_space=pltpu.VMEM),
        ],
        out_specs=pl.BlockSpec(memory_space=pltpu.VMEM),
        scratch_shapes=[
            pltpu.VMEM((TICKS, npad, rows, BLK), jnp.bfloat16),
            pltpu.SemaphoreType.DMA((TICKS, n_chunk, 3)),
            pltpu.SemaphoreType.DMA((TICKS, n_chunk, 3)),
            pltpu.SemaphoreType.DMA((3,)),
        ] + [pltpu.VMEM((npad, rows // n_chunk, BLK), jnp.bfloat16) for _ in range(n_chunk)],
        compiler_params=pltpu.CompilerParams(
            collective_id=0, has_side_effects=True, vmem_limit_bytes=48 * 1024 * 1024),
    )(cols, pend, w, bias)
    return out.transpose(0, 2, 1, 3).reshape(TICKS, rows, nb * BLK)


def solution(mesh):
    n_sec = mesh.shape["section"]
    n_blk = mesh.shape["blk"]
    in_specs = (
        P("section", "blk"),
        P("section", "blk", None, None, None),
        P("section", "blk", None),
        P("section", "blk"),
    )
    out_specs = P(None, "section", "blk")
    return jax.shard_map(functools.partial(shards, n_sec, n_blk, ROW_CHUNKS), mesh=mesh, in_specs=in_specs,
                         out_specs=out_specs, check_vma=False)
```

```python
import functools

import jax
import jax.numpy as jnp
from jax import lax
from jax.experimental import pallas as pl
from jax.experimental.pallas import tpu as pltpu
from jax.sharding import PartitionSpec as P

BLK = 128
HALO = 4
TICKS = 8
ROW_CHUNKS = 4
MESH = pl.DeviceIdType.MESH


def relay_kernel(n_sec, n_blk, n_chunk, cols_ref, pend_ref, w_ref, b_ref, out_ref,
                 slots, send_sem, recv_sem, local_sem, *works):
    s = lax.axis_index("section")
    d = lax.axis_index("blk")
    nb = pend_ref.shape[0]
    rc = pend_ref.shape[1] // n_chunk
    left = lax.rem(d + n_blk - 1, n_blk)
    right = lax.rem(d + 1, n_blk)
    s_next = jnp.minimum(s + 1, n_sec - 1)
    s_prev = jnp.maximum(s - 1, 0)

    barrier = pltpu.get_barrier_semaphore()
    for nd in (left, right):
        pl.semaphore_signal(barrier, inc=1, device_id=(s, nd), device_id_type=MESH)

    @pl.when(s < n_sec - 1)
    def _():
        for nd in (left, d, right):
            pl.semaphore_signal(barrier, inc=1, device_id=(s_next, nd), device_id_type=MESH)

    @pl.when(s > 0)
    def _():
        for nd in (left, d, right):
            pl.semaphore_signal(barrier, inc=1, device_id=(s_prev, nd), device_id_type=MESH)

    has_prev = (s + n_sec - 1) // n_sec
    has_next = (2 * n_sec - 3 - s) // (n_sec - 1)
    pl.semaphore_wait(barrier, 2 + 3 * has_prev + 3 * has_next)

    def copies(src, t, c, tgt_sec):
        rows = pl.ds(c * rc, rc)
        center = pltpu.make_async_remote_copy(
            src_ref=src.at[:, rows],
            dst_ref=slots.at[t, pl.ds(HALO, nb), rows],
            send_sem=send_sem.at[t, c, 0], recv_sem=recv_sem.at[t, c, 0],
            device_id=(tgt_sec, d), device_id_type=MESH)
        lo = pltpu.make_async_remote_copy(
            src_ref=src.at[pl.ds(0, HALO), rows],
            dst_ref=slots.at[t, pl.ds(HALO + nb, HALO), rows],
            send_sem=send_sem.at[t, c, 1], recv_sem=recv_sem.at[t, c, 1],
            device_id=(tgt_sec, left), device_id_type=MESH)
        hi = pltpu.make_async_remote_copy(
            src_ref=src.at[pl.ds(nb - HALO, HALO), rows],
            dst_ref=slots.at[t, pl.ds(0, HALO), rows],
            send_sem=send_sem.at[t, c, 2], recv_sem=recv_sem.at[t, c, 2],
            device_id=(tgt_sec, right), device_id_type=MESH)
        return center, lo, hi

    first = [copies(pend_ref, 0, c, s)[1:] for c in range(n_chunk)]
    for pair in first:
        for cp in pair:
            cp.start()
    for c in range(n_chunk):
        rows = pl.ds(c * rc, rc)
        own = pltpu.make_async_copy(pend_ref.at[:, rows], works[c].at[pl.ds(HALO, nb)], local_sem.at[0])
        own.start()
        own.wait()
        for cp in first[c]:
            cp.wait_recv()
        cp_lo = pltpu.make_async_copy(slots.at[0, pl.ds(0, HALO), rows], works[c].at[pl.ds(0, HALO)],
                                      local_sem.at[1])
        cp_hi = pltpu.make_async_copy(slots.at[0, pl.ds(HALO + nb, HALO), rows],
                                      works[c].at[pl.ds(HALO + nb, HALO)], local_sem.at[2])
        cp_lo.start()
        cp_hi.start()
        cp_lo.wait()
        cp_hi.wait()

    def compute(t, c):
        work = works[c]

        def row_body(i, carry):
            xs = [work[cols_ref[i, k]] for k in range(w_ref.shape[1] // BLK)]
            xcat = jnp.concatenate(xs, axis=1)
            acc = jnp.dot(xcat, w_ref[i], preferred_element_type=jnp.float32)
            acc = acc + b_ref[i]
            out_ref[t, i, pl.ds(c * rc, rc)] = jnp.maximum(acc, 0.0).astype(out_ref.dtype)
            return carry
        lax.fori_loop(0, nb, row_body, 0)

    for t in range(TICKS):
        for c in range(n_chunk):
            if t > 0:
                @pl.when(s >= t)
                def _():
                    for cp in copies(out_ref.at[t - 1], t, c, s):
                        cp.wait_recv()
                    cw = pltpu.make_async_copy(slots.at[t, :, pl.ds(c * rc, rc)], works[c], local_sem.at[0])
                    cw.start()
                    cw.wait()

            @pl.when(s >= t)
            def _():
                compute(t, c)

            @pl.when(s < t)
            def _():
                out_ref[t, :, pl.ds(c * rc, rc)] = jnp.zeros((nb, rc, BLK), out_ref.dtype)

            if t + 1 < TICKS:
                @pl.when((s >= t) & (s < n_sec - 1))
                def _():
                    for cp in copies(out_ref.at[t], t + 1, c, s_next):
                        cp.start()

    for pair in first:
        for cp in pair:
            cp.wait_send()
    for t in range(TICKS - 1):
        @pl.when((s >= t) & (s < n_sec - 1))
        def _():
            for c in range(n_chunk):
                for cp in copies(out_ref.at[t], t + 1, c, s_next):
                    cp.wait_send()


def shards(n_sec, n_blk, n_chunk, pending_groups, coefficient_tiles, source_block_indices, additive_offsets):
    rows, units = pending_groups.shape
    nb = coefficient_tiles.shape[1]
    nz = coefficient_tiles.shape[2]
    d = lax.axis_index("blk")
    cols = jnp.mod(source_block_indices[0] - d * nb + HALO, nb * n_blk).astype(jnp.int32)
    pend = pending_groups.reshape(rows, nb, BLK).transpose(1, 0, 2)
    w = coefficient_tiles[0].reshape(nb, nz * BLK, BLK)
    bias = additive_offsets[0].reshape(nb, 1, BLK)
    npad = nb + 2 * HALO
    out = pl.pallas_call(
        functools.partial(relay_kernel, n_sec, n_blk, n_chunk),
        out_shape=jax.ShapeDtypeStruct((TICKS, nb, rows, BLK), jnp.bfloat16),
        in_specs=[
            pl.BlockSpec(memory_space=pltpu.SMEM),
            pl.BlockSpec(memory_space=pltpu.VMEM),
            pl.BlockSpec(memory_space=pltpu.VMEM),
            pl.BlockSpec(memory_space=pltpu.VMEM),
        ],
        out_specs=pl.BlockSpec(memory_space=pltpu.VMEM),
        scratch_shapes=[
            pltpu.VMEM((TICKS, npad, rows, BLK), jnp.bfloat16),
            pltpu.SemaphoreType.DMA((TICKS, n_chunk, 3)),
            pltpu.SemaphoreType.DMA((TICKS, n_chunk, 3)),
            pltpu.SemaphoreType.DMA((3,)),
        ] + [pltpu.VMEM((npad, rows // n_chunk, BLK), jnp.bfloat16) for _ in range(n_chunk)],
        compiler_params=pltpu.CompilerParams(
            collective_id=0, has_side_effects=True, vmem_limit_bytes=48 * 1024 * 1024),
    )(cols, pend, w, bias)
    return out.transpose(0, 2, 1, 3).reshape(TICKS, rows, nb * BLK)


def solution(mesh):
    n_sec = mesh.shape["section"]
    n_blk = mesh.shape["blk"]
    in_specs = (
        P("section", "blk"),
        P("section", "blk", None, None, None),
        P("section", "blk", None),
        P("section", "blk"),
    )
    out_specs = P(None, "section", "blk")
    return jax.shard_map(functools.partial(shards, n_sec, n_blk, ROW_CHUNKS), mesh=mesh, in_specs=in_specs,
                         out_specs=out_specs, check_vma=False)
```

```python
import functools

import jax
import jax.numpy as jnp
from jax import lax
from jax.experimental import pallas as pl
from jax.experimental.pallas import tpu as pltpu
from jax.sharding import PartitionSpec as P

BLK = 128
HALO = 4
TICKS = 8
ROW_CHUNKS = 2
MESH = pl.DeviceIdType.MESH


def relay_kernel(n_sec, n_blk, n_chunk, cols_ref, pend_ref, w_ref, b_ref, out_ref,
                 slots, send_sem, recv_sem, local_sem, *works):
    s = lax.axis_index("section")
    d = lax.axis_index("blk")
    nb = pend_ref.shape[0]
    rc = pend_ref.shape[1] // n_chunk
    left = lax.rem(d + n_blk - 1, n_blk)
    right = lax.rem(d + 1, n_blk)
    s_next = jnp.minimum(s + 1, n_sec - 1)
    s_prev = jnp.maximum(s - 1, 0)

    barrier = pltpu.get_barrier_semaphore()
    for nd in (left, right):
        pl.semaphore_signal(barrier, inc=1, device_id=(s, nd), device_id_type=MESH)

    @pl.when(s < n_sec - 1)
    def _():
        for nd in (left, d, right):
            pl.semaphore_signal(barrier, inc=1, device_id=(s_next, nd), device_id_type=MESH)

    @pl.when(s > 0)
    def _():
        for nd in (left, d, right):
            pl.semaphore_signal(barrier, inc=1, device_id=(s_prev, nd), device_id_type=MESH)

    has_prev = (s + n_sec - 1) // n_sec
    has_next = (2 * n_sec - 3 - s) // (n_sec - 1)
    pl.semaphore_wait(barrier, 2 + 3 * has_prev + 3 * has_next)

    def copies(src, t, c, tgt_sec):
        rows = pl.ds(c * rc, rc)
        center = pltpu.make_async_remote_copy(
            src_ref=src.at[:, rows],
            dst_ref=slots.at[t, pl.ds(HALO, nb), rows],
            send_sem=send_sem.at[t, c, 0], recv_sem=recv_sem.at[t, c, 0],
            device_id=(tgt_sec, d), device_id_type=MESH)
        lo = pltpu.make_async_remote_copy(
            src_ref=src.at[pl.ds(0, HALO), rows],
            dst_ref=slots.at[t, pl.ds(HALO + nb, HALO), rows],
            send_sem=send_sem.at[t, c, 1], recv_sem=recv_sem.at[t, c, 1],
            device_id=(tgt_sec, left), device_id_type=MESH)
        hi = pltpu.make_async_remote_copy(
            src_ref=src.at[pl.ds(nb - HALO, HALO), rows],
            dst_ref=slots.at[t, pl.ds(0, HALO), rows],
            send_sem=send_sem.at[t, c, 2], recv_sem=recv_sem.at[t, c, 2],
            device_id=(tgt_sec, right), device_id_type=MESH)
        return center, lo, hi

    first = [copies(pend_ref, 0, c, s)[1:] for c in range(n_chunk)]
    for pair in first:
        for cp in pair:
            cp.start()
    for c in range(n_chunk):
        rows = pl.ds(c * rc, rc)
        own = pltpu.make_async_copy(pend_ref.at[:, rows], works[c].at[pl.ds(HALO, nb)], local_sem.at[0])
        own.start()
        own.wait()
        for cp in first[c]:
            cp.wait_recv()
        cp_lo = pltpu.make_async_copy(slots.at[0, pl.ds(0, HALO), rows], works[c].at[pl.ds(0, HALO)],
                                      local_sem.at[1])
        cp_hi = pltpu.make_async_copy(slots.at[0, pl.ds(HALO + nb, HALO), rows],
                                      works[c].at[pl.ds(HALO + nb, HALO)], local_sem.at[2])
        cp_lo.start()
        cp_hi.start()
        cp_lo.wait()
        cp_hi.wait()

    def compute(t, c):
        work = works[c]

        def row_body(i, carry):
            xs = [work[cols_ref[i, k]] for k in range(w_ref.shape[1] // BLK)]
            xcat = jnp.concatenate(xs, axis=1)
            acc = jnp.dot(xcat, w_ref[i], preferred_element_type=jnp.float32)
            acc = acc + b_ref[i]
            out_ref[t, i, pl.ds(c * rc, rc)] = jnp.maximum(acc, 0.0).astype(out_ref.dtype)
            return carry
        lax.fori_loop(0, nb, row_body, 0, unroll=8)

    for t in range(TICKS):
        for c in range(n_chunk):
            if t > 0:
                @pl.when(s >= t)
                def _():
                    for cp in copies(out_ref.at[t - 1], t, c, s):
                        cp.wait_recv()
                    cw = pltpu.make_async_copy(slots.at[t, :, pl.ds(c * rc, rc)], works[c], local_sem.at[0])
                    cw.start()
                    cw.wait()

            @pl.when(s >= t)
            def _():
                compute(t, c)

            @pl.when(s < t)
            def _():
                out_ref[t, :, pl.ds(c * rc, rc)] = jnp.zeros((nb, rc, BLK), out_ref.dtype)

            if t + 1 < TICKS:
                @pl.when((s >= t) & (s < n_sec - 1))
                def _():
                    for cp in copies(out_ref.at[t], t + 1, c, s_next):
                        cp.start()

    for pair in first:
        for cp in pair:
            cp.wait_send()
    for t in range(TICKS - 1):
        @pl.when((s >= t) & (s < n_sec - 1))
        def _():
            for c in range(n_chunk):
                for cp in copies(out_ref.at[t], t + 1, c, s_next):
                    cp.wait_send()


def shards(n_sec, n_blk, n_chunk, pending_groups, coefficient_tiles, source_block_indices, additive_offsets):
    rows, units = pending_groups.shape
    nb = coefficient_tiles.shape[1]
    nz = coefficient_tiles.shape[2]
    d = lax.axis_index("blk")
    cols = jnp.mod(source_block_indices[0] - d * nb + HALO, nb * n_blk).astype(jnp.int32)
    pend = pending_groups.reshape(rows, nb, BLK).transpose(1, 0, 2)
    w = coefficient_tiles[0].reshape(nb, nz * BLK, BLK)
    bias = additive_offsets[0].reshape(nb, 1, BLK)
    npad = nb + 2 * HALO
    out = pl.pallas_call(
        functools.partial(relay_kernel, n_sec, n_blk, n_chunk),
        out_shape=jax.ShapeDtypeStruct((TICKS, nb, rows, BLK), jnp.bfloat16),
        in_specs=[
            pl.BlockSpec(memory_space=pltpu.SMEM),
            pl.BlockSpec(memory_space=pltpu.VMEM),
            pl.BlockSpec(memory_space=pltpu.VMEM),
            pl.BlockSpec(memory_space=pltpu.VMEM),
        ],
        out_specs=pl.BlockSpec(memory_space=pltpu.VMEM),
        scratch_shapes=[
            pltpu.VMEM((TICKS, npad, rows, BLK), jnp.bfloat16),
            pltpu.SemaphoreType.DMA((TICKS, n_chunk, 3)),
            pltpu.SemaphoreType.DMA((TICKS, n_chunk, 3)),
            pltpu.SemaphoreType.DMA((3,)),
        ] + [pltpu.VMEM((npad, rows // n_chunk, BLK), jnp.bfloat16) for _ in range(n_chunk)],
        compiler_params=pltpu.CompilerParams(
            collective_id=0, has_side_effects=True, vmem_limit_bytes=48 * 1024 * 1024),
    )(cols, pend, w, bias)
    return out.transpose(0, 2, 1, 3).reshape(TICKS, rows, nb * BLK)


def solution(mesh):
    n_sec = mesh.shape["section"]
    n_blk = mesh.shape["blk"]
    in_specs = (
        P("section", "blk"),
        P("section", "blk", None, None, None),
        P("section", "blk", None),
        P("section", "blk"),
    )
    out_specs = P(None, "section", "blk")
    return jax.shard_map(functools.partial(shards, n_sec, n_blk, ROW_CHUNKS), mesh=mesh, in_specs=in_specs,
                         out_specs=out_specs, check_vma=False)
```

```python
import functools

import jax
import jax.numpy as jnp
from jax import lax
from jax.experimental import pallas as pl
from jax.experimental.pallas import tpu as pltpu
from jax.sharding import PartitionSpec as P

BLK = 128
HALO = 4
TICKS = 8
ROW_CHUNKS = 2
MESH = pl.DeviceIdType.MESH


def relay_kernel(n_sec, n_blk, n_chunk, cols_ref, pend_ref, w_ref, b_ref, out_ref,
                 slots, send_sem, recv_sem, local_sem, *works):
    s = lax.axis_index("section")
    d = lax.axis_index("blk")
    nb = pend_ref.shape[0]
    rc = pend_ref.shape[1] // n_chunk
    left = lax.rem(d + n_blk - 1, n_blk)
    right = lax.rem(d + 1, n_blk)
    s_next = jnp.minimum(s + 1, n_sec - 1)
    s_prev = jnp.maximum(s - 1, 0)

    barrier = pltpu.get_barrier_semaphore()
    for nd in (left, right):
        pl.semaphore_signal(barrier, inc=1, device_id=(s, nd), device_id_type=MESH)

    @pl.when(s < n_sec - 1)
    def _():
        pl.semaphore_signal(barrier, inc=1, device_id=(s_next, d), device_id_type=MESH)

    @pl.when(s > 0)
    def _():
        pl.semaphore_signal(barrier, inc=1, device_id=(s_prev, d), device_id_type=MESH)

    has_prev = (s + n_sec - 1) // n_sec
    has_next = (2 * n_sec - 3 - s) // (n_sec - 1)
    pl.semaphore_wait(barrier, 2 + has_prev + has_next)

    def center_copy(t, c):
        rows = pl.ds(c * rc, rc)
        return pltpu.make_async_remote_copy(
            src_ref=out_ref.at[t - 1, :, rows],
            dst_ref=slots.at[t, pl.ds(HALO, nb), rows],
            send_sem=send_sem.at[t, c, 0], recv_sem=recv_sem.at[t, c, 0],
            device_id=(s_next, d), device_id_type=MESH)

    def edge_copies(src, t, c):
        rows = pl.ds(c * rc, rc)
        lo = pltpu.make_async_remote_copy(
            src_ref=src.at[pl.ds(0, HALO), rows],
            dst_ref=slots.at[t, pl.ds(HALO + nb, HALO), rows],
            send_sem=send_sem.at[t, c, 1], recv_sem=recv_sem.at[t, c, 1],
            device_id=(s, left), device_id_type=MESH)
        hi = pltpu.make_async_remote_copy(
            src_ref=src.at[pl.ds(nb - HALO, HALO), rows],
            dst_ref=slots.at[t, pl.ds(0, HALO), rows],
            send_sem=send_sem.at[t, c, 2], recv_sem=recv_sem.at[t, c, 2],
            device_id=(s, right), device_id_type=MESH)
        return lo, hi

    first = [edge_copies(pend_ref, 0, c) for c in range(n_chunk)]
    for pair in first:
        for cp in pair:
            cp.start()
    for c in range(n_chunk):
        rows = pl.ds(c * rc, rc)
        own = pltpu.make_async_copy(pend_ref.at[:, rows], works[c].at[pl.ds(HALO, nb)], local_sem.at[0])
        own.start()
        own.wait()
        for cp in first[c]:
            cp.wait_recv()
        cp_lo = pltpu.make_async_copy(slots.at[0, pl.ds(0, HALO), rows], works[c].at[pl.ds(0, HALO)],
                                      local_sem.at[1])
        cp_hi = pltpu.make_async_copy(slots.at[0, pl.ds(HALO + nb, HALO), rows],
                                      works[c].at[pl.ds(HALO + nb, HALO)], local_sem.at[2])
        cp_lo.start()
        cp_hi.start()
        cp_lo.wait()
        cp_hi.wait()

    def compute(t, c):
        work = works[c]

        def row_body(i, carry):
            xs = [work[cols_ref[i, k]] for k in range(w_ref.shape[1] // BLK)]
            xcat = jnp.concatenate(xs, axis=1)
            acc = jnp.dot(xcat, w_ref[i], preferred_element_type=jnp.float32)
            acc = acc + b_ref[i]
            out_ref[t, i, pl.ds(c * rc, rc)] = jnp.maximum(acc, 0.0).astype(out_ref.dtype)
            return carry
        lax.fori_loop(0, nb, row_body, 0, unroll=8)

    for t in range(TICKS):
        for c in range(n_chunk):
            if t > 0:
                @pl.when(s >= t)
                def _():
                    center_copy(t, c).wait_recv()
                    fwd = edge_copies(slots.at[t, pl.ds(HALO, nb)], t, c)
                    for cp in fwd:
                        cp.start()
                    for cp in fwd:
                        cp.wait_recv()
                    cw = pltpu.make_async_copy(slots.at[t, :, pl.ds(c * rc, rc)], works[c], local_sem.at[0])
                    cw.start()
                    cw.wait()

            @pl.when(s >= t)
            def _():
                compute(t, c)

            @pl.when(s < t)
            def _():
                out_ref[t, :, pl.ds(c * rc, rc)] = jnp.zeros((nb, rc, BLK), out_ref.dtype)

            if t + 1 < TICKS:
                @pl.when((s >= t) & (s < n_sec - 1))
                def _():
                    center_copy(t + 1, c).start()

    for pair in first:
        for cp in pair:
            cp.wait_send()
    for t in range(TICKS - 1):
        @pl.when((s >= t) & (s < n_sec - 1))
        def _():
            for c in range(n_chunk):
                center_copy(t + 1, c).wait_send()
    for t in range(1, TICKS):
        @pl.when(s >= t)
        def _():
            for c in range(n_chunk):
                for cp in edge_copies(slots.at[t, pl.ds(HALO, nb)], t, c):
                    cp.wait_send()


def shards(n_sec, n_blk, n_chunk, pending_groups, coefficient_tiles, source_block_indices, additive_offsets):
    rows, units = pending_groups.shape
    nb = coefficient_tiles.shape[1]
    nz = coefficient_tiles.shape[2]
    d = lax.axis_index("blk")
    cols = jnp.mod(source_block_indices[0] - d * nb + HALO, nb * n_blk).astype(jnp.int32)
    pend = pending_groups.reshape(rows, nb, BLK).transpose(1, 0, 2)
    w = coefficient_tiles[0].reshape(nb, nz * BLK, BLK)
    bias = additive_offsets[0].reshape(nb, 1, BLK)
    npad = nb + 2 * HALO
    out = pl.pallas_call(
        functools.partial(relay_kernel, n_sec, n_blk, n_chunk),
        out_shape=jax.ShapeDtypeStruct((TICKS, nb, rows, BLK), jnp.bfloat16),
        in_specs=[
            pl.BlockSpec(memory_space=pltpu.SMEM),
            pl.BlockSpec(memory_space=pltpu.VMEM),
            pl.BlockSpec(memory_space=pltpu.VMEM),
            pl.BlockSpec(memory_space=pltpu.VMEM),
        ],
        out_specs=pl.BlockSpec(memory_space=pltpu.VMEM),
        scratch_shapes=[
            pltpu.VMEM((TICKS, npad, rows, BLK), jnp.bfloat16),
            pltpu.SemaphoreType.DMA((TICKS, n_chunk, 3)),
            pltpu.SemaphoreType.DMA((TICKS, n_chunk, 3)),
            pltpu.SemaphoreType.DMA((3,)),
        ] + [pltpu.VMEM((npad, rows // n_chunk, BLK), jnp.bfloat16) for _ in range(n_chunk)],
        compiler_params=pltpu.CompilerParams(
            collective_id=0, has_side_effects=True, vmem_limit_bytes=48 * 1024 * 1024),
    )(cols, pend, w, bias)
    return out.transpose(0, 2, 1, 3).reshape(TICKS, rows, nb * BLK)


def solution(mesh):
    n_sec = mesh.shape["section"]
    n_blk = mesh.shape["blk"]
    in_specs = (
        P("section", "blk"),
        P("section", "blk", None, None, None),
        P("section", "blk", None),
        P("section", "blk"),
    )
    out_specs = P(None, "section", "blk")
    return jax.shard_map(functools.partial(shards, n_sec, n_blk, ROW_CHUNKS), mesh=mesh, in_specs=in_specs,
                         out_specs=out_specs, check_vma=False)
```

```python
import functools

import jax
import jax.numpy as jnp
from jax import lax
from jax.experimental import pallas as pl
from jax.experimental.pallas import tpu as pltpu
from jax.sharding import PartitionSpec as P

BLK = 128
HALO = 4
TICKS = 8
ROW_CHUNKS = 2
W_PIECES = 4
MESH = pl.DeviceIdType.MESH


def relay_kernel(n_sec, n_blk, n_chunk, cols_ref, pend_ref, w_hbm, b_ref, out_ref,
                 w_ref, w_sem, slots, send_sem, recv_sem, local_sem, *works):
    n_piece = w_sem.shape[0]
    per_piece = w_hbm.shape[0] // n_piece
    w_copies = [pltpu.make_async_copy(w_hbm.at[pl.ds(j * per_piece, per_piece)],
                                      w_ref.at[pl.ds(j * per_piece, per_piece)], w_sem.at[j])
                for j in range(n_piece)]
    for cp in w_copies:
        cp.start()
    s = lax.axis_index("section")
    d = lax.axis_index("blk")
    nb = pend_ref.shape[0]
    rc = pend_ref.shape[1] // n_chunk
    left = lax.rem(d + n_blk - 1, n_blk)
    right = lax.rem(d + 1, n_blk)
    s_next = jnp.minimum(s + 1, n_sec - 1)
    s_prev = jnp.maximum(s - 1, 0)

    barrier = pltpu.get_barrier_semaphore()
    for nd in (left, right):
        pl.semaphore_signal(barrier, inc=1, device_id=(s, nd), device_id_type=MESH)

    @pl.when(s < n_sec - 1)
    def _():
        pl.semaphore_signal(barrier, inc=1, device_id=(s_next, d), device_id_type=MESH)

    @pl.when(s > 0)
    def _():
        pl.semaphore_signal(barrier, inc=1, device_id=(s_prev, d), device_id_type=MESH)

    has_prev = (s + n_sec - 1) // n_sec
    has_next = (2 * n_sec - 3 - s) // (n_sec - 1)
    pl.semaphore_wait(barrier, 2 + has_prev + has_next)

    def center_copy(t, c):
        rows = pl.ds(c * rc, rc)
        return pltpu.make_async_remote_copy(
            src_ref=out_ref.at[t - 1, :, rows],
            dst_ref=slots.at[t, pl.ds(HALO, nb), rows],
            send_sem=send_sem.at[t, c, 0], recv_sem=recv_sem.at[t, c, 0],
            device_id=(s_next, d), device_id_type=MESH)

    def edge_copies(src, t, c):
        rows = pl.ds(c * rc, rc)
        lo = pltpu.make_async_remote_copy(
            src_ref=src.at[pl.ds(0, HALO), rows],
            dst_ref=slots.at[t, pl.ds(HALO + nb, HALO), rows],
            send_sem=send_sem.at[t, c, 1], recv_sem=recv_sem.at[t, c, 1],
            device_id=(s, left), device_id_type=MESH)
        hi = pltpu.make_async_remote_copy(
            src_ref=src.at[pl.ds(nb - HALO, HALO), rows],
            dst_ref=slots.at[t, pl.ds(0, HALO), rows],
            send_sem=send_sem.at[t, c, 2], recv_sem=recv_sem.at[t, c, 2],
            device_id=(s, right), device_id_type=MESH)
        return lo, hi

    first = [edge_copies(pend_ref, 0, c) for c in range(n_chunk)]
    for pair in first:
        for cp in pair:
            cp.start()
    for c in range(n_chunk):
        rows = pl.ds(c * rc, rc)
        own = pltpu.make_async_copy(pend_ref.at[:, rows], works[c].at[pl.ds(HALO, nb)], local_sem.at[0])
        own.start()
        own.wait()
        for cp in first[c]:
            cp.wait_recv()
        cp_lo = pltpu.make_async_copy(slots.at[0, pl.ds(0, HALO), rows], works[c].at[pl.ds(0, HALO)],
                                      local_sem.at[1])
        cp_hi = pltpu.make_async_copy(slots.at[0, pl.ds(HALO + nb, HALO), rows],
                                      works[c].at[pl.ds(HALO + nb, HALO)], local_sem.at[2])
        cp_lo.start()
        cp_hi.start()
        cp_lo.wait()
        cp_hi.wait()

    def compute(t, c):
        work = works[c]

        def row_body(i, carry):
            xs = [work[cols_ref[i, k]] for k in range(w_ref.shape[1] // BLK)]
            xcat = jnp.concatenate(xs, axis=1)
            acc = jnp.dot(xcat, w_ref[i], preferred_element_type=jnp.float32)
            acc = acc + b_ref[i]
            out_ref[t, i, pl.ds(c * rc, rc)] = jnp.maximum(acc, 0.0).astype(out_ref.dtype)
            return carry
        if t == 0 and c == 0:
            for j in range(n_piece):
                w_copies[j].wait()
                lax.fori_loop(j * per_piece, (j + 1) * per_piece, row_body, 0, unroll=8)
        else:
            lax.fori_loop(0, nb, row_body, 0, unroll=8)

    for t in range(TICKS):
        for c in range(n_chunk):
            if t > 0:
                @pl.when(s >= t)
                def _():
                    center_copy(t, c).wait_recv()
                    fwd = edge_copies(slots.at[t, pl.ds(HALO, nb)], t, c)
                    for cp in fwd:
                        cp.start()
                    for cp in fwd:
                        cp.wait_recv()
                    cw = pltpu.make_async_copy(slots.at[t, :, pl.ds(c * rc, rc)], works[c], local_sem.at[0])
                    cw.start()
                    cw.wait()

            @pl.when(s >= t)
            def _():
                compute(t, c)

            @pl.when(s < t)
            def _():
                out_ref[t, :, pl.ds(c * rc, rc)] = jnp.zeros((nb, rc, BLK), out_ref.dtype)

            if t + 1 < TICKS:
                @pl.when((s >= t) & (s < n_sec - 1))
                def _():
                    center_copy(t + 1, c).start()

    for pair in first:
        for cp in pair:
            cp.wait_send()
    for t in range(TICKS - 1):
        @pl.when((s >= t) & (s < n_sec - 1))
        def _():
            for c in range(n_chunk):
                center_copy(t + 1, c).wait_send()
    for t in range(1, TICKS):
        @pl.when(s >= t)
        def _():
            for c in range(n_chunk):
                for cp in edge_copies(slots.at[t, pl.ds(HALO, nb)], t, c):
                    cp.wait_send()


def shards(n_sec, n_blk, n_chunk, pending_groups, coefficient_tiles, source_block_indices, additive_offsets):
    rows, units = pending_groups.shape
    nb = coefficient_tiles.shape[1]
    nz = coefficient_tiles.shape[2]
    d = lax.axis_index("blk")
    cols = jnp.mod(source_block_indices[0] - d * nb + HALO, nb * n_blk).astype(jnp.int32)
    pend = pending_groups.reshape(rows, nb, BLK).transpose(1, 0, 2)
    w = coefficient_tiles[0].reshape(nb, nz * BLK, BLK)
    bias = additive_offsets[0].reshape(nb, 1, BLK)
    npad = nb + 2 * HALO
    out = pl.pallas_call(
        functools.partial(relay_kernel, n_sec, n_blk, n_chunk),
        out_shape=jax.ShapeDtypeStruct((TICKS, nb, rows, BLK), jnp.bfloat16),
        in_specs=[
            pl.BlockSpec(memory_space=pltpu.SMEM),
            pl.BlockSpec(memory_space=pltpu.VMEM),
            pl.BlockSpec(memory_space=pl.ANY),
            pl.BlockSpec(memory_space=pltpu.VMEM),
        ],
        out_specs=pl.BlockSpec(memory_space=pltpu.VMEM),
        scratch_shapes=[
            pltpu.VMEM((nb, nz * BLK, BLK), jnp.bfloat16),
            pltpu.SemaphoreType.DMA((W_PIECES,)),
            pltpu.VMEM((TICKS, npad, rows, BLK), jnp.bfloat16),
            pltpu.SemaphoreType.DMA((TICKS, n_chunk, 3)),
            pltpu.SemaphoreType.DMA((TICKS, n_chunk, 3)),
            pltpu.SemaphoreType.DMA((3,)),
        ] + [pltpu.VMEM((npad, rows // n_chunk, BLK), jnp.bfloat16) for _ in range(n_chunk)],
        compiler_params=pltpu.CompilerParams(
            collective_id=0, has_side_effects=True, vmem_limit_bytes=48 * 1024 * 1024),
    )(cols, pend, w, bias)
    return out.transpose(0, 2, 1, 3).reshape(TICKS, rows, nb * BLK)


def solution(mesh):
    n_sec = mesh.shape["section"]
    n_blk = mesh.shape["blk"]
    in_specs = (
        P("section", "blk"),
        P("section", "blk", None, None, None),
        P("section", "blk", None),
        P("section", "blk"),
    )
    out_specs = P(None, "section", "blk")
    return jax.shard_map(functools.partial(shards, n_sec, n_blk, ROW_CHUNKS), mesh=mesh, in_specs=in_specs,
                         out_specs=out_specs, check_vma=False)
```

```python
import functools

import jax
import jax.numpy as jnp
from jax import lax
from jax.experimental import pallas as pl
from jax.experimental.pallas import tpu as pltpu
from jax.sharding import PartitionSpec as P

BLK = 128
HALO = 4
TICKS = 8
ROW_CHUNKS = 2
W_PIECES = 4
MESH = pl.DeviceIdType.MESH


def relay_kernel(n_sec, n_blk, n_chunk, src_ref, pend_ref, w_hbm, b_hbm, out_ref,
                 w_ref, w_sem, b_ref, sendbuf, slots, send_sem, recv_sem, local_sem, *works):
    n_piece = w_sem.shape[0]
    per_piece = w_hbm.shape[0] // n_piece
    w_copies = [pltpu.make_async_copy(w_hbm.at[pl.ds(j * per_piece, per_piece)],
                                      w_ref.at[pl.ds(j * per_piece, per_piece)], w_sem.at[j])
                for j in range(n_piece)]
    b_copy = pltpu.make_async_copy(b_hbm, b_ref, local_sem.at[3])
    b_copy.start()
    for cp in w_copies:
        cp.start()
    s = lax.axis_index("section")
    d = lax.axis_index("blk")
    nb = pend_ref.shape[0]
    rc = pend_ref.shape[1] // n_chunk
    left = lax.rem(d + n_blk - 1, n_blk)
    right = lax.rem(d + 1, n_blk)
    s_next = jnp.minimum(s + 1, n_sec - 1)
    s_prev = jnp.maximum(s - 1, 0)

    n_cols = nb * n_blk
    col_shift = n_cols - d * nb + HALO
    n_pad = nb + 2 * HALO
    barrier = pltpu.get_barrier_semaphore()
    for nd in (left, right):
        pl.semaphore_signal(barrier, inc=1, device_id=(s, nd), device_id_type=MESH)

    @pl.when(s < n_sec - 1)
    def _():
        pl.semaphore_signal(barrier, inc=1, device_id=(s_next, d), device_id_type=MESH)

    @pl.when(s > 0)
    def _():
        pl.semaphore_signal(barrier, inc=1, device_id=(s_prev, d), device_id_type=MESH)

    has_prev = (s + n_sec - 1) // n_sec
    has_next = (2 * n_sec - 3 - s) // (n_sec - 1)
    pl.semaphore_wait(barrier, 2 + has_prev + has_next)

    def center_copy(t, c):
        rows = pl.ds(c * rc, rc)
        return pltpu.make_async_remote_copy(
            src_ref=sendbuf.at[t - 1, :, rows],
            dst_ref=slots.at[t, pl.ds(HALO, nb), rows],
            send_sem=send_sem.at[t, c, 0], recv_sem=recv_sem.at[t, c, 0],
            device_id=(s_next, d), device_id_type=MESH)

    def edge_copies(src, t, c):
        rows = pl.ds(c * rc, rc)
        lo = pltpu.make_async_remote_copy(
            src_ref=src.at[pl.ds(0, HALO), rows],
            dst_ref=slots.at[t, pl.ds(HALO + nb, HALO), rows],
            send_sem=send_sem.at[t, c, 1], recv_sem=recv_sem.at[t, c, 1],
            device_id=(s, left), device_id_type=MESH)
        hi = pltpu.make_async_remote_copy(
            src_ref=src.at[pl.ds(nb - HALO, HALO), rows],
            dst_ref=slots.at[t, pl.ds(0, HALO), rows],
            send_sem=send_sem.at[t, c, 2], recv_sem=recv_sem.at[t, c, 2],
            device_id=(s, right), device_id_type=MESH)
        return lo, hi

    first = [edge_copies(pend_ref, 0, c) for c in range(n_chunk)]
    for pair in first:
        for cp in pair:
            cp.start()
    for c in range(n_chunk):
        rows = pl.ds(c * rc, rc)
        own = pltpu.make_async_copy(pend_ref.at[:, rows], works[c].at[pl.ds(HALO, nb)], local_sem.at[0])
        own.start()
        own.wait()
        for cp in first[c]:
            cp.wait_recv()
        cp_lo = pltpu.make_async_copy(slots.at[0, pl.ds(0, HALO), rows], works[c].at[pl.ds(0, HALO)],
                                      local_sem.at[1])
        cp_hi = pltpu.make_async_copy(slots.at[0, pl.ds(HALO + nb, HALO), rows],
                                      works[c].at[pl.ds(HALO + nb, HALO)], local_sem.at[2])
        cp_lo.start()
        cp_hi.start()
        cp_lo.wait()
        cp_hi.wait()

    def compute(t, c):
        work = works[c]

        def row_body(i, carry):
            xs = [work[jnp.minimum(lax.rem(src_ref[i, k] + col_shift, n_cols), n_pad - 1)]
                  for k in range(w_ref.shape[1] // BLK)]
            xcat = jnp.concatenate(xs, axis=1)
            acc = jnp.dot(xcat, w_ref[i], preferred_element_type=jnp.float32)
            acc = acc + b_ref[i]
            y = jnp.maximum(acc, 0.0).astype(out_ref.dtype)
            sendbuf[t, i, pl.ds(c * rc, rc)] = y
            out_ref[t, pl.ds(c * rc, rc), pl.ds(pl.multiple_of(i * BLK, BLK), BLK)] = y
            return carry
        if t == 0 and c == 0:
            b_copy.wait()
            for j in range(n_piece):
                w_copies[j].wait()
                lax.fori_loop(j * per_piece, (j + 1) * per_piece, row_body, 0, unroll=8)
        else:
            lax.fori_loop(0, nb, row_body, 0, unroll=8)

    for t in range(TICKS):
        for c in range(n_chunk):
            if t > 0:
                @pl.when(s >= t)
                def _():
                    center_copy(t, c).wait_recv()
                    fwd = edge_copies(slots.at[t, pl.ds(HALO, nb)], t, c)
                    for cp in fwd:
                        cp.start()
                    for cp in fwd:
                        cp.wait_recv()
                    cw = pltpu.make_async_copy(slots.at[t, :, pl.ds(c * rc, rc)], works[c], local_sem.at[0])
                    cw.start()
                    cw.wait()

            @pl.when(s >= t)
            def _():
                compute(t, c)

            @pl.when(s < t)
            def _():
                out_ref[t, pl.ds(c * rc, rc)] = jnp.zeros((rc, nb * BLK), out_ref.dtype)

            if t + 1 < TICKS:
                @pl.when((s >= t) & (s < n_sec - 1))
                def _():
                    center_copy(t + 1, c).start()

    for pair in first:
        for cp in pair:
            cp.wait_send()
    for t in range(TICKS - 1):
        @pl.when((s >= t) & (s < n_sec - 1))
        def _():
            for c in range(n_chunk):
                center_copy(t + 1, c).wait_send()
    for t in range(1, TICKS):
        @pl.when(s >= t)
        def _():
            for c in range(n_chunk):
                for cp in edge_copies(slots.at[t, pl.ds(HALO, nb)], t, c):
                    cp.wait_send()


def shards(n_sec, n_blk, n_chunk, pending_groups, coefficient_tiles, source_block_indices, additive_offsets):
    rows, units = pending_groups.shape
    nb = coefficient_tiles.shape[1]
    nz = coefficient_tiles.shape[2]
    pend = pending_groups.reshape(rows, nb, BLK).transpose(1, 0, 2)
    w = coefficient_tiles[0].reshape(nb, nz * BLK, BLK)
    bias = additive_offsets[0].reshape(nb, 1, BLK)
    npad = nb + 2 * HALO
    return pl.pallas_call(
        functools.partial(relay_kernel, n_sec, n_blk, n_chunk),
        out_shape=jax.ShapeDtypeStruct((TICKS, rows, nb * BLK), jnp.bfloat16),
        in_specs=[
            pl.BlockSpec(memory_space=pltpu.SMEM),
            pl.BlockSpec(memory_space=pltpu.VMEM),
            pl.BlockSpec(memory_space=pl.ANY),
            pl.BlockSpec(memory_space=pl.ANY),
        ],
        out_specs=pl.BlockSpec(memory_space=pltpu.VMEM),
        scratch_shapes=[
            pltpu.VMEM((nb, nz * BLK, BLK), jnp.bfloat16),
            pltpu.SemaphoreType.DMA((W_PIECES,)),
            pltpu.VMEM((nb, 1, BLK), jnp.float32),
            pltpu.VMEM((TICKS, nb, rows, BLK), jnp.bfloat16),
            pltpu.VMEM((TICKS, npad, rows, BLK), jnp.bfloat16),
            pltpu.SemaphoreType.DMA((TICKS, n_chunk, 3)),
            pltpu.SemaphoreType.DMA((TICKS, n_chunk, 3)),
            pltpu.SemaphoreType.DMA((4,)),
        ] + [pltpu.VMEM((npad, rows // n_chunk, BLK), jnp.bfloat16) for _ in range(n_chunk)],
        compiler_params=pltpu.CompilerParams(
            collective_id=0, has_side_effects=True, vmem_limit_bytes=48 * 1024 * 1024),
    )(source_block_indices[0], pend, w, bias)


def solution(mesh):
    n_sec = mesh.shape["section"]
    n_blk = mesh.shape["blk"]
    in_specs = (
        P("section", "blk"),
        P("section", "blk", None, None, None),
        P("section", "blk", None),
        P("section", "blk"),
    )
    out_specs = P(None, "section", "blk")
    return jax.shard_map(functools.partial(shards, n_sec, n_blk, ROW_CHUNKS), mesh=mesh, in_specs=in_specs,
                         out_specs=out_specs, check_vma=False)
```

```python
import functools

import jax
import jax.numpy as jnp
from jax import lax
from jax.experimental import pallas as pl
from jax.experimental.pallas import tpu as pltpu
from jax.sharding import PartitionSpec as P

BLK = 128
HALO = 4
TICKS = 8
ROW_CHUNKS = 2
W_PIECES = 4
MESH = pl.DeviceIdType.MESH


def relay_kernel(n_sec, n_blk, n_chunk, src_ref, pend_ref, w_hbm, b_hbm, out_ref,
                 w_ref, w_sem, b_ref, sendbuf, slots, send_sem, recv_sem, local_sem, *works):
    n_piece = w_sem.shape[0]
    per_piece = w_hbm.shape[0] // n_piece
    w_copies = [pltpu.make_async_copy(w_hbm.at[pl.ds(j * per_piece, per_piece)],
                                      w_ref.at[pl.ds(j * per_piece, per_piece)], w_sem.at[j])
                for j in range(n_piece)]
    b_copy = pltpu.make_async_copy(b_hbm, b_ref, local_sem.at[3])
    b_copy.start()
    for cp in w_copies:
        cp.start()
    s = lax.axis_index("section")
    d = lax.axis_index("blk")
    nb = pend_ref.shape[0]
    rc = pend_ref.shape[1] // n_chunk
    left = lax.rem(d + n_blk - 1, n_blk)
    right = lax.rem(d + 1, n_blk)
    s_next = jnp.minimum(s + 1, n_sec - 1)
    s_prev = jnp.maximum(s - 1, 0)

    n_cols = nb * n_blk
    col_shift = n_cols - d * nb + HALO
    n_pad = nb + 2 * HALO
    barrier = pltpu.get_barrier_semaphore()
    for nd in (left, right):
        pl.semaphore_signal(barrier, inc=1, device_id=(s, nd), device_id_type=MESH)

    @pl.when(s < n_sec - 1)
    def _():
        pl.semaphore_signal(barrier, inc=1, device_id=(s_next, d), device_id_type=MESH)

    @pl.when(s > 0)
    def _():
        pl.semaphore_signal(barrier, inc=1, device_id=(s_prev, d), device_id_type=MESH)

    has_prev = (s + n_sec - 1) // n_sec
    has_next = (2 * n_sec - 3 - s) // (n_sec - 1)
    pl.semaphore_wait(barrier, 2 + has_prev + has_next)

    def center_copies(t, c):
        rows = pl.ds(c * rc, rc)
        parts = ((3, 0, HALO), (4, nb - HALO, HALO), (0, HALO, nb - 2 * HALO))
        return [pltpu.make_async_remote_copy(
            src_ref=sendbuf.at[t - 1, pl.ds(lo, n), rows],
            dst_ref=slots.at[t, pl.ds(HALO + lo, n), rows],
            send_sem=send_sem.at[t, c, j], recv_sem=recv_sem.at[t, c, j],
            device_id=(s_next, d), device_id_type=MESH) for j, lo, n in parts]

    def edge_copies(src, t, c):
        rows = pl.ds(c * rc, rc)
        lo = pltpu.make_async_remote_copy(
            src_ref=src.at[pl.ds(0, HALO), rows],
            dst_ref=slots.at[t, pl.ds(HALO + nb, HALO), rows],
            send_sem=send_sem.at[t, c, 1], recv_sem=recv_sem.at[t, c, 1],
            device_id=(s, left), device_id_type=MESH)
        hi = pltpu.make_async_remote_copy(
            src_ref=src.at[pl.ds(nb - HALO, HALO), rows],
            dst_ref=slots.at[t, pl.ds(0, HALO), rows],
            send_sem=send_sem.at[t, c, 2], recv_sem=recv_sem.at[t, c, 2],
            device_id=(s, right), device_id_type=MESH)
        return lo, hi

    first = [edge_copies(pend_ref, 0, c) for c in range(n_chunk)]
    for pair in first:
        for cp in pair:
            cp.start()
    for c in range(n_chunk):
        rows = pl.ds(c * rc, rc)
        own = pltpu.make_async_copy(pend_ref.at[:, rows], works[c].at[pl.ds(HALO, nb)], local_sem.at[0])
        own.start()
        own.wait()
        for cp in first[c]:
            cp.wait_recv()
        cp_lo = pltpu.make_async_copy(slots.at[0, pl.ds(0, HALO), rows], works[c].at[pl.ds(0, HALO)],
                                      local_sem.at[1])
        cp_hi = pltpu.make_async_copy(slots.at[0, pl.ds(HALO + nb, HALO), rows],
                                      works[c].at[pl.ds(HALO + nb, HALO)], local_sem.at[2])
        cp_lo.start()
        cp_hi.start()
        cp_lo.wait()
        cp_hi.wait()

    def compute(t, c):
        work = works[c]

        def row_body(i, carry):
            xs = [work[jnp.minimum(lax.rem(src_ref[i, k] + col_shift, n_cols), n_pad - 1)]
                  for k in range(w_ref.shape[1] // BLK)]
            xcat = jnp.concatenate(xs, axis=1)
            acc = jnp.dot(xcat, w_ref[i], preferred_element_type=jnp.float32)
            acc = acc + b_ref[i]
            y = jnp.maximum(acc, 0.0).astype(out_ref.dtype)
            sendbuf[t, i, pl.ds(c * rc, rc)] = y
            out_ref[t, pl.ds(c * rc, rc), pl.ds(pl.multiple_of(i * BLK, BLK), BLK)] = y
            return carry
        if t == 0 and c == 0:
            b_copy.wait()
            for j in range(n_piece):
                w_copies[j].wait()
                lax.fori_loop(j * per_piece, (j + 1) * per_piece, row_body, 0, unroll=8)
        else:
            lax.fori_loop(0, nb, row_body, 0, unroll=8)

    for t in range(TICKS):
        for c in range(n_chunk):
            if t > 0:
                @pl.when(s >= t)
                def _():
                    parts = center_copies(t, c)
                    parts[0].wait_recv()
                    parts[1].wait_recv()
                    fwd = edge_copies(slots.at[t, pl.ds(HALO, nb)], t, c)
                    for cp in fwd:
                        cp.start()
                    parts[2].wait_recv()
                    for cp in fwd:
                        cp.wait_recv()
                    cw = pltpu.make_async_copy(slots.at[t, :, pl.ds(c * rc, rc)], works[c], local_sem.at[0])
                    cw.start()
                    cw.wait()

            @pl.when(s >= t)
            def _():
                compute(t, c)

            @pl.when(s < t)
            def _():
                out_ref[t, pl.ds(c * rc, rc)] = jnp.zeros((rc, nb * BLK), out_ref.dtype)

            if t + 1 < TICKS:
                @pl.when((s >= t) & (s < n_sec - 1))
                def _():
                    for cp in center_copies(t + 1, c):
                        cp.start()

    for pair in first:
        for cp in pair:
            cp.wait_send()
    for t in range(TICKS - 1):
        @pl.when((s >= t) & (s < n_sec - 1))
        def _():
            for c in range(n_chunk):
                for cp in center_copies(t + 1, c):
                    cp.wait_send()
    for t in range(1, TICKS):
        @pl.when(s >= t)
        def _():
            for c in range(n_chunk):
                for cp in edge_copies(slots.at[t, pl.ds(HALO, nb)], t, c):
                    cp.wait_send()


def shards(n_sec, n_blk, n_chunk, pending_groups, coefficient_tiles, source_block_indices, additive_offsets):
    rows, units = pending_groups.shape
    nb = coefficient_tiles.shape[1]
    nz = coefficient_tiles.shape[2]
    pend = pending_groups.reshape(rows, nb, BLK).transpose(1, 0, 2)
    w = coefficient_tiles[0].reshape(nb, nz * BLK, BLK)
    bias = additive_offsets[0].reshape(nb, 1, BLK)
    npad = nb + 2 * HALO
    return pl.pallas_call(
        functools.partial(relay_kernel, n_sec, n_blk, n_chunk),
        out_shape=jax.ShapeDtypeStruct((TICKS, rows, nb * BLK), jnp.bfloat16),
        in_specs=[
            pl.BlockSpec(memory_space=pltpu.SMEM),
            pl.BlockSpec(memory_space=pltpu.VMEM),
            pl.BlockSpec(memory_space=pl.ANY),
            pl.BlockSpec(memory_space=pl.ANY),
        ],
        out_specs=pl.BlockSpec(memory_space=pltpu.VMEM),
        scratch_shapes=[
            pltpu.VMEM((nb, nz * BLK, BLK), jnp.bfloat16),
            pltpu.SemaphoreType.DMA((W_PIECES,)),
            pltpu.VMEM((nb, 1, BLK), jnp.float32),
            pltpu.VMEM((TICKS, nb, rows, BLK), jnp.bfloat16),
            pltpu.VMEM((TICKS, npad, rows, BLK), jnp.bfloat16),
            pltpu.SemaphoreType.DMA((TICKS, n_chunk, 5)),
            pltpu.SemaphoreType.DMA((TICKS, n_chunk, 5)),
            pltpu.SemaphoreType.DMA((4,)),
        ] + [pltpu.VMEM((npad, rows // n_chunk, BLK), jnp.bfloat16) for _ in range(n_chunk)],
        compiler_params=pltpu.CompilerParams(
            collective_id=0, has_side_effects=True, vmem_limit_bytes=48 * 1024 * 1024),
    )(source_block_indices[0], pend, w, bias)


def solution(mesh):
    n_sec = mesh.shape["section"]
    n_blk = mesh.shape["blk"]
    in_specs = (
        P("section", "blk"),
        P("section", "blk", None, None, None),
        P("section", "blk", None),
        P("section", "blk"),
    )
    out_specs = P(None, "section", "blk")
    return jax.shard_map(functools.partial(shards, n_sec, n_blk, ROW_CHUNKS), mesh=mesh, in_specs=in_specs,
                         out_specs=out_specs, check_vma=False)
```

```python
import functools

import jax
import jax.numpy as jnp
from jax import lax
from jax.experimental import pallas as pl
from jax.experimental.pallas import tpu as pltpu
from jax.sharding import PartitionSpec as P

BLK = 128
HALO = 4
TICKS = 8
ROW_CHUNKS = 2
W_PIECES = 4
MESH = pl.DeviceIdType.MESH


def relay_kernel(n_sec, n_blk, n_chunk, src_ref, pend_ref, w_hbm, b_hbm, out_ref,
                 w_ref, w_sem, b_ref, sendbuf, send_sem, recv_sem, local_sem, *slot_list):
    n_piece = w_sem.shape[0]
    per_piece = w_hbm.shape[0] // n_piece
    w_copies = [pltpu.make_async_copy(w_hbm.at[pl.ds(j * per_piece, per_piece)],
                                      w_ref.at[pl.ds(j * per_piece, per_piece)], w_sem.at[j])
                for j in range(n_piece)]
    b_copy = pltpu.make_async_copy(b_hbm, b_ref, local_sem.at[3])
    b_copy.start()
    for cp in w_copies:
        cp.start()
    slots = [slot_list[t * n_chunk:(t + 1) * n_chunk] for t in range(TICKS)]
    s = lax.axis_index("section")
    d = lax.axis_index("blk")
    nb = pend_ref.shape[0]
    rc = pend_ref.shape[1] // n_chunk
    left = lax.rem(d + n_blk - 1, n_blk)
    right = lax.rem(d + 1, n_blk)
    s_next = jnp.minimum(s + 1, n_sec - 1)
    s_prev = jnp.maximum(s - 1, 0)

    n_cols = nb * n_blk
    col_shift = n_cols - d * nb + HALO
    n_pad = nb + 2 * HALO
    barrier = pltpu.get_barrier_semaphore()
    for nd in (left, right):
        pl.semaphore_signal(barrier, inc=1, device_id=(s, nd), device_id_type=MESH)

    @pl.when(s < n_sec - 1)
    def _():
        pl.semaphore_signal(barrier, inc=1, device_id=(s_next, d), device_id_type=MESH)

    @pl.when(s > 0)
    def _():
        pl.semaphore_signal(barrier, inc=1, device_id=(s_prev, d), device_id_type=MESH)

    has_prev = (s + n_sec - 1) // n_sec
    has_next = (2 * n_sec - 3 - s) // (n_sec - 1)
    pl.semaphore_wait(barrier, 2 + has_prev + has_next)

    def center_copies(t, c):
        rows = pl.ds(c * rc, rc)
        parts = ((3, 0, HALO), (4, nb - HALO, HALO), (0, HALO, nb - 2 * HALO))
        return [pltpu.make_async_remote_copy(
            src_ref=sendbuf.at[t - 1, pl.ds(lo, n), rows],
            dst_ref=slots[t][c].at[pl.ds(HALO + lo, n)],
            send_sem=send_sem.at[t, c, j], recv_sem=recv_sem.at[t, c, j],
            device_id=(s_next, d), device_id_type=MESH) for j, lo, n in parts]

    def edge_copies(src, t, c):
        lo = pltpu.make_async_remote_copy(
            src_ref=src.at[pl.ds(0, HALO)],
            dst_ref=slots[t][c].at[pl.ds(HALO + nb, HALO)],
            send_sem=send_sem.at[t, c, 1], recv_sem=recv_sem.at[t, c, 1],
            device_id=(s, left), device_id_type=MESH)
        hi = pltpu.make_async_remote_copy(
            src_ref=src.at[pl.ds(nb - HALO, HALO)],
            dst_ref=slots[t][c].at[pl.ds(0, HALO)],
            send_sem=send_sem.at[t, c, 2], recv_sem=recv_sem.at[t, c, 2],
            device_id=(s, right), device_id_type=MESH)
        return lo, hi

    first = [edge_copies(pend_ref.at[:, pl.ds(c * rc, rc)], 0, c) for c in range(n_chunk)]
    for pair in first:
        for cp in pair:
            cp.start()
    for c in range(n_chunk):
        own = pltpu.make_async_copy(pend_ref.at[:, pl.ds(c * rc, rc)], slots[0][c].at[pl.ds(HALO, nb)],
                                    local_sem.at[0])
        own.start()
        own.wait()
        for cp in first[c]:
            cp.wait_recv()

    def compute(t, c):
        work = slots[t][c]

        def row_body(i, carry):
            xs = [work[jnp.minimum(lax.rem(src_ref[i, k] + col_shift, n_cols), n_pad - 1)]
                  for k in range(w_ref.shape[1] // BLK)]
            xcat = jnp.concatenate(xs, axis=1)
            acc = jnp.dot(xcat, w_ref[i], preferred_element_type=jnp.float32)
            acc = acc + b_ref[i]
            y = jnp.maximum(acc, 0.0).astype(out_ref.dtype)
            sendbuf[t, i, pl.ds(c * rc, rc)] = y
            out_ref[t, pl.ds(c * rc, rc), pl.ds(pl.multiple_of(i * BLK, BLK), BLK)] = y
            return carry
        if t == 0 and c == 0:
            b_copy.wait()
            for j in range(n_piece):
                w_copies[j].wait()
                lax.fori_loop(j * per_piece, (j + 1) * per_piece, row_body, 0, unroll=8)
        else:
            lax.fori_loop(0, nb, row_body, 0, unroll=8)

    for t in range(TICKS):
        for c in range(n_chunk):
            if t > 0:
                @pl.when(s >= t)
                def _():
                    parts = center_copies(t, c)
                    parts[0].wait_recv()
                    parts[1].wait_recv()
                    fwd = edge_copies(slots[t][c].at[pl.ds(HALO, nb)], t, c)
                    for cp in fwd:
                        cp.start()
                    parts[2].wait_recv()
                    for cp in fwd:
                        cp.wait_recv()

            @pl.when(s >= t)
            def _():
                compute(t, c)

            @pl.when(s < t)
            def _():
                out_ref[t, pl.ds(c * rc, rc)] = jnp.zeros((rc, nb * BLK), out_ref.dtype)

            if t + 1 < TICKS:
                @pl.when((s >= t) & (s < n_sec - 1))
                def _():
                    for cp in center_copies(t + 1, c):
                        cp.start()

    for pair in first:
        for cp in pair:
            cp.wait_send()
    for t in range(TICKS - 1):
        @pl.when((s >= t) & (s < n_sec - 1))
        def _():
            for c in range(n_chunk):
                for cp in center_copies(t + 1, c):
                    cp.wait_send()
    for t in range(1, TICKS):
        @pl.when(s >= t)
        def _():
            for c in range(n_chunk):
                for cp in edge_copies(slots[t][c].at[pl.ds(HALO, nb)], t, c):
                    cp.wait_send()


def shards(n_sec, n_blk, n_chunk, pending_groups, coefficient_tiles, source_block_indices, additive_offsets):
    rows, units = pending_groups.shape
    nb = coefficient_tiles.shape[1]
    nz = coefficient_tiles.shape[2]
    pend = pending_groups.reshape(rows, nb, BLK).transpose(1, 0, 2)
    w = coefficient_tiles[0].reshape(nb, nz * BLK, BLK)
    bias = additive_offsets[0].reshape(nb, 1, BLK)
    npad = nb + 2 * HALO
    return pl.pallas_call(
        functools.partial(relay_kernel, n_sec, n_blk, n_chunk),
        out_shape=jax.ShapeDtypeStruct((TICKS, rows, nb * BLK), jnp.bfloat16),
        in_specs=[
            pl.BlockSpec(memory_space=pltpu.SMEM),
            pl.BlockSpec(memory_space=pltpu.VMEM),
            pl.BlockSpec(memory_space=pl.ANY),
            pl.BlockSpec(memory_space=pl.ANY),
        ],
        out_specs=pl.BlockSpec(memory_space=pltpu.VMEM),
        scratch_shapes=[
            pltpu.VMEM((nb, nz * BLK, BLK), jnp.bfloat16),
            pltpu.SemaphoreType.DMA((W_PIECES,)),
            pltpu.VMEM((nb, 1, BLK), jnp.float32),
            pltpu.VMEM((TICKS, nb, rows, BLK), jnp.bfloat16),
            pltpu.SemaphoreType.DMA((TICKS, n_chunk, 5)),
            pltpu.SemaphoreType.DMA((TICKS, n_chunk, 5)),
            pltpu.SemaphoreType.DMA((4,)),
        ] + [pltpu.VMEM((npad, rows // n_chunk, BLK), jnp.bfloat16) for _ in range(TICKS * n_chunk)],
        compiler_params=pltpu.CompilerParams(
            collective_id=0, has_side_effects=True, vmem_limit_bytes=48 * 1024 * 1024),
    )(source_block_indices[0], pend, w, bias)


def solution(mesh):
    n_sec = mesh.shape["section"]
    n_blk = mesh.shape["blk"]
    in_specs = (
        P("section", "blk"),
        P("section", "blk", None, None, None),
        P("section", "blk", None),
        P("section", "blk"),
    )
    out_specs = P(None, "section", "blk")
    return jax.shard_map(functools.partial(shards, n_sec, n_blk, ROW_CHUNKS), mesh=mesh, in_specs=in_specs,
                         out_specs=out_specs, check_vma=False)
```

```python
import functools

import jax
import jax.numpy as jnp
from jax import lax
from jax.experimental import pallas as pl
from jax.experimental.pallas import tpu as pltpu
from jax.sharding import PartitionSpec as P

BLK = 128
HALO = 4
TICKS = 8
ROW_CHUNKS = 2
W_PIECES = 4
VMEM_BYTES = 67043328
MESH = pl.DeviceIdType.MESH


def relay_kernel(n_sec, n_blk, n_chunk, src_ref, pend_ref, w_hbm, b_hbm, out_ref,
                 w_ref, w_sem, b_ref, sendbuf, send_sem, recv_sem, local_sem, *slot_list):
    n_piece = w_sem.shape[0]
    per_piece = w_hbm.shape[0] // n_piece
    w_copies = [pltpu.make_async_copy(w_hbm.at[pl.ds(j * per_piece, per_piece)],
                                      w_ref.at[pl.ds(j * per_piece, per_piece)], w_sem.at[j])
                for j in range(n_piece)]
    b_copy = pltpu.make_async_copy(b_hbm, b_ref, local_sem.at[3])
    b_copy.start()
    for cp in w_copies:
        cp.start()
    slots = [slot_list[t * n_chunk:(t + 1) * n_chunk] for t in range(TICKS)]
    s = lax.axis_index("section")
    d = lax.axis_index("blk")
    nb = pend_ref.shape[0]
    rc = pend_ref.shape[1] // n_chunk
    left = lax.rem(d + n_blk - 1, n_blk)
    right = lax.rem(d + 1, n_blk)
    s_next = jnp.minimum(s + 1, n_sec - 1)
    s_prev = jnp.maximum(s - 1, 0)

    n_cols = nb * n_blk
    col_shift = n_cols - d * nb + HALO
    n_pad = nb + 2 * HALO
    barrier = pltpu.get_barrier_semaphore()
    for nd in (left, right):
        pl.semaphore_signal(barrier, inc=1, device_id=(s, nd), device_id_type=MESH)

    @pl.when(s < n_sec - 1)
    def _():
        pl.semaphore_signal(barrier, inc=1, device_id=(s_next, d), device_id_type=MESH)

    @pl.when(s > 0)
    def _():
        pl.semaphore_signal(barrier, inc=1, device_id=(s_prev, d), device_id_type=MESH)

    has_prev = (s + n_sec - 1) // n_sec
    has_next = (2 * n_sec - 3 - s) // (n_sec - 1)
    pl.semaphore_wait(barrier, 2 + has_prev + has_next)

    def center_copies(t, c):
        rows = pl.ds(c * rc, rc)
        parts = ((3, 0, HALO), (4, nb - HALO, HALO), (0, HALO, nb - 2 * HALO))
        return [pltpu.make_async_remote_copy(
            src_ref=sendbuf.at[t - 1, pl.ds(lo, n), rows],
            dst_ref=slots[t][c].at[pl.ds(HALO + lo, n)],
            send_sem=send_sem.at[t, c, j], recv_sem=recv_sem.at[t, c, j],
            device_id=(s_next, d), device_id_type=MESH) for j, lo, n in parts]

    def edge_copies(src, t, c):
        lo = pltpu.make_async_remote_copy(
            src_ref=src.at[pl.ds(0, HALO)],
            dst_ref=slots[t][c].at[pl.ds(HALO + nb, HALO)],
            send_sem=send_sem.at[t, c, 1], recv_sem=recv_sem.at[t, c, 1],
            device_id=(s, left), device_id_type=MESH)
        hi = pltpu.make_async_remote_copy(
            src_ref=src.at[pl.ds(nb - HALO, HALO)],
            dst_ref=slots[t][c].at[pl.ds(0, HALO)],
            send_sem=send_sem.at[t, c, 2], recv_sem=recv_sem.at[t, c, 2],
            device_id=(s, right), device_id_type=MESH)
        return lo, hi

    first = [edge_copies(pend_ref.at[:, pl.ds(c * rc, rc)], 0, c) for c in range(n_chunk)]
    for pair in first:
        for cp in pair:
            cp.start()
    for c in range(n_chunk):
        own = pltpu.make_async_copy(pend_ref.at[:, pl.ds(c * rc, rc)], slots[0][c].at[pl.ds(HALO, nb)],
                                    local_sem.at[0])
        own.start()
        own.wait()
        for cp in first[c]:
            cp.wait_recv()

    def compute(t, c):
        work = slots[t][c]

        def row_body(i, carry):
            xs = [work[jnp.minimum(lax.rem(src_ref[k, i] + col_shift, n_cols), n_pad - 1)]
                  for k in range(w_ref.shape[1] // BLK)]
            xcat = jnp.concatenate(xs, axis=1)
            acc = jnp.dot(xcat, w_ref[i], preferred_element_type=jnp.float32)
            acc = acc + b_ref[i]
            y = jnp.maximum(acc, 0.0).astype(out_ref.dtype)
            sendbuf[t, i, pl.ds(c * rc, rc)] = y
            out_ref[t, pl.ds(c * rc, rc), pl.ds(pl.multiple_of(i * BLK, BLK), BLK)] = y
            return carry
        if t == 0 and c == 0:
            b_copy.wait()
            for j in range(n_piece):
                w_copies[j].wait()
                lax.fori_loop(j * per_piece, (j + 1) * per_piece, row_body, 0, unroll=8)
        else:
            lax.fori_loop(0, nb, row_body, 0, unroll=8)

    for t in range(TICKS):
        for c in range(n_chunk):
            if t > 0:
                @pl.when(s >= t)
                def _():
                    parts = center_copies(t, c)
                    parts[0].wait_recv()
                    parts[1].wait_recv()
                    fwd = edge_copies(slots[t][c].at[pl.ds(HALO, nb)], t, c)
                    for cp in fwd:
                        cp.start()
                    parts[2].wait_recv()
                    for cp in fwd:
                        cp.wait_recv()

            @pl.when(s >= t)
            def _():
                compute(t, c)

            @pl.when(s < t)
            def _():
                out_ref[t, pl.ds(c * rc, rc)] = jnp.zeros((rc, nb * BLK), out_ref.dtype)

            if t + 1 < TICKS:
                @pl.when((s >= t) & (s < n_sec - 1))
                def _():
                    for cp in center_copies(t + 1, c):
                        cp.start()

    for pair in first:
        for cp in pair:
            cp.wait_send()
    for t in range(TICKS - 1):
        @pl.when((s >= t) & (s < n_sec - 1))
        def _():
            for c in range(n_chunk):
                for cp in center_copies(t + 1, c):
                    cp.wait_send()
    for t in range(1, TICKS):
        @pl.when(s >= t)
        def _():
            for c in range(n_chunk):
                for cp in edge_copies(slots[t][c].at[pl.ds(HALO, nb)], t, c):
                    cp.wait_send()


def shards(n_sec, n_blk, n_chunk, pending_groups, coefficient_tiles, source_block_indices, additive_offsets):
    rows, units = pending_groups.shape
    nb = coefficient_tiles.shape[1]
    nz = coefficient_tiles.shape[2]
    pend = pending_groups.reshape(rows, nb, BLK).transpose(1, 0, 2)
    w = coefficient_tiles[0].reshape(nb, nz * BLK, BLK)
    bias = additive_offsets[0].reshape(nb, 1, BLK)
    npad = nb + 2 * HALO
    return pl.pallas_call(
        functools.partial(relay_kernel, n_sec, n_blk, n_chunk),
        out_shape=jax.ShapeDtypeStruct((TICKS, rows, nb * BLK), jnp.bfloat16),
        in_specs=[
            pl.BlockSpec(memory_space=pltpu.SMEM),
            pl.BlockSpec(memory_space=pltpu.VMEM),
            pl.BlockSpec(memory_space=pl.ANY),
            pl.BlockSpec(memory_space=pl.ANY),
        ],
        out_specs=pl.BlockSpec(memory_space=pltpu.VMEM),
        scratch_shapes=[
            pltpu.VMEM((nb, nz * BLK, BLK), jnp.bfloat16),
            pltpu.SemaphoreType.DMA((W_PIECES,)),
            pltpu.VMEM((nb, 1, BLK), jnp.float32),
            pltpu.VMEM((TICKS, nb, rows, BLK), jnp.bfloat16),
            pltpu.SemaphoreType.DMA((TICKS, n_chunk, 5)),
            pltpu.SemaphoreType.DMA((TICKS, n_chunk, 5)),
            pltpu.SemaphoreType.DMA((4,)),
        ] + [pltpu.VMEM((npad, rows // n_chunk, BLK), jnp.bfloat16) for _ in range(TICKS * n_chunk)],
        compiler_params=pltpu.CompilerParams(
            collective_id=0, has_side_effects=True, vmem_limit_bytes=VMEM_BYTES),
    )(source_block_indices[0].T, pend, w, bias)


def solution(mesh):
    n_sec = mesh.shape["section"]
    n_blk = mesh.shape["blk"]
    in_specs = (
        P("section", "blk"),
        P("section", "blk", None, None, None),
        P("section", "blk", None),
        P("section", "blk"),
    )
    out_specs = P(None, "section", "blk")
    return jax.shard_map(functools.partial(shards, n_sec, n_blk, ROW_CHUNKS), mesh=mesh, in_specs=in_specs,
                         out_specs=out_specs, check_vma=False)
```

```python
import functools

import jax
import jax.numpy as jnp
from jax import lax
from jax.experimental import pallas as pl
from jax.experimental.pallas import tpu as pltpu
from jax.sharding import PartitionSpec as P

BLK = 128
HALO = 4
TICKS = 8
ROW_CHUNKS = 2
W_PIECES = 4
VMEM_BYTES = 48 * 1024 * 1024
MESH = pl.DeviceIdType.MESH


def relay_kernel(n_sec, n_blk, n_chunk, src_ref, pend_ref, w_hbm, b_hbm, out_ref,
                 w_ref, w_sem, b_ref, sendbuf, send_sem, recv_sem, local_sem, *slot_list):
    n_piece = w_sem.shape[0]
    per_piece = w_hbm.shape[0] // n_piece
    w_copies = [pltpu.make_async_copy(w_hbm.at[pl.ds(j * per_piece, per_piece)],
                                      w_ref.at[pl.ds(j * per_piece, per_piece)], w_sem.at[j])
                for j in range(n_piece)]
    b_copy = pltpu.make_async_copy(b_hbm, b_ref, local_sem.at[3])
    b_copy.start()
    for cp in w_copies:
        cp.start()
    slots = [slot_list[t * n_chunk:(t + 1) * n_chunk] for t in range(TICKS)]
    s = lax.axis_index("section")
    d = lax.axis_index("blk")
    nb = pend_ref.shape[0]
    rc = pend_ref.shape[1] // n_chunk
    left = lax.rem(d + n_blk - 1, n_blk)
    right = lax.rem(d + 1, n_blk)
    s_next = jnp.minimum(s + 1, n_sec - 1)
    s_prev = jnp.maximum(s - 1, 0)

    n_cols = nb * n_blk
    col_shift = n_cols - d * nb + HALO
    n_pad = nb + 2 * HALO
    barrier = pltpu.get_barrier_semaphore()
    for nd in (left, right):
        pl.semaphore_signal(barrier, inc=1, device_id=(s, nd), device_id_type=MESH)

    @pl.when(s < n_sec - 1)
    def _():
        pl.semaphore_signal(barrier, inc=1, device_id=(s_next, d), device_id_type=MESH)

    @pl.when(s > 0)
    def _():
        pl.semaphore_signal(barrier, inc=1, device_id=(s_prev, d), device_id_type=MESH)

    has_prev = (s + n_sec - 1) // n_sec
    has_next = (2 * n_sec - 3 - s) // (n_sec - 1)
    pl.semaphore_wait(barrier, 2 + has_prev + has_next)

    def center_copies(t, c):
        rows = pl.ds(c * rc, rc)
        parts = ((3, 0, HALO), (4, nb - HALO, HALO), (0, HALO, nb - 2 * HALO))
        return [pltpu.make_async_remote_copy(
            src_ref=sendbuf.at[t - 1, pl.ds(lo, n), rows],
            dst_ref=slots[t][c].at[pl.ds(HALO + lo, n)],
            send_sem=send_sem.at[t, c, j], recv_sem=recv_sem.at[t, c, j],
            device_id=(s_next, d), device_id_type=MESH) for j, lo, n in parts]

    def edge_copies(src, t, c):
        lo = pltpu.make_async_remote_copy(
            src_ref=src.at[pl.ds(0, HALO)],
            dst_ref=slots[t][c].at[pl.ds(HALO + nb, HALO)],
            send_sem=send_sem.at[t, c, 1], recv_sem=recv_sem.at[t, c, 1],
            device_id=(s, left), device_id_type=MESH)
        hi = pltpu.make_async_remote_copy(
            src_ref=src.at[pl.ds(nb - HALO, HALO)],
            dst_ref=slots[t][c].at[pl.ds(0, HALO)],
            send_sem=send_sem.at[t, c, 2], recv_sem=recv_sem.at[t, c, 2],
            device_id=(s, right), device_id_type=MESH)
        return lo, hi

    first = [edge_copies(pend_ref.at[:, pl.ds(c * rc, rc)], 0, c) for c in range(n_chunk)]
    for pair in first:
        for cp in pair:
            cp.start()
    for c in range(n_chunk):
        own = pltpu.make_async_copy(pend_ref.at[:, pl.ds(c * rc, rc)], slots[0][c].at[pl.ds(HALO, nb)],
                                    local_sem.at[0])
        own.start()
        own.wait()
        for cp in first[c]:
            cp.wait_recv()

    def compute(t, c):
        work = slots[t][c]

        def row_body(i, carry):
            xs = [work[jnp.minimum(lax.rem(src_ref[k, i] + col_shift, n_cols), n_pad - 1)]
                  for k in range(w_ref.shape[1] // BLK)]
            xcat = jnp.concatenate(xs, axis=1)
            acc = jnp.dot(xcat, w_ref[i], preferred_element_type=jnp.float32)
            acc = acc + b_ref[i]
            y = jnp.maximum(acc, 0.0).astype(out_ref.dtype)
            sendbuf[t, i, pl.ds(c * rc, rc)] = y
            out_ref[t, pl.ds(c * rc, rc), pl.ds(pl.multiple_of(i * BLK, BLK), BLK)] = y
            return carry
        if t == 0 and c == 0:
            b_copy.wait()
            for j in range(n_piece):
                w_copies[j].wait()
                lax.fori_loop(j * per_piece, (j + 1) * per_piece, row_body, 0, unroll=8)
        else:
            lax.fori_loop(0, nb, row_body, 0, unroll=8)

    for t in range(TICKS):
        for c in range(n_chunk):
            if t > 0:
                @pl.when(s >= t)
                def _():
                    parts = center_copies(t, c)
                    parts[0].wait_recv()
                    parts[1].wait_recv()
                    fwd = edge_copies(slots[t][c].at[pl.ds(HALO, nb)], t, c)
                    for cp in fwd:
                        cp.start()
                    parts[2].wait_recv()
                    for cp in fwd:
                        cp.wait_recv()

            @pl.when(s >= t)
            def _():
                compute(t, c)

            @pl.when(s < t)
            def _():
                out_ref[t, pl.ds(c * rc, rc)] = jnp.zeros((rc, nb * BLK), out_ref.dtype)

            if t + 1 < TICKS:
                @pl.when((s >= t) & (s < n_sec - 1))
                def _():
                    for cp in center_copies(t + 1, c):
                        cp.start()

    for pair in first:
        for cp in pair:
            cp.wait_send()
    for t in range(TICKS - 1):
        @pl.when((s >= t) & (s < n_sec - 1))
        def _():
            for c in range(n_chunk):
                for cp in center_copies(t + 1, c):
                    cp.wait_send()
    for t in range(1, TICKS):
        @pl.when(s >= t)
        def _():
            for c in range(n_chunk):
                for cp in edge_copies(slots[t][c].at[pl.ds(HALO, nb)], t, c):
                    cp.wait_send()


def shards(n_sec, n_blk, n_chunk, pending_groups, coefficient_tiles, source_block_indices, additive_offsets):
    rows, units = pending_groups.shape
    nb = coefficient_tiles.shape[1]
    nz = coefficient_tiles.shape[2]
    pend = pending_groups.reshape(rows, nb, BLK).transpose(1, 0, 2)
    w = coefficient_tiles[0].reshape(nb, nz * BLK, BLK)
    bias = additive_offsets[0].reshape(nb, 1, BLK)
    npad = nb + 2 * HALO
    return pl.pallas_call(
        functools.partial(relay_kernel, n_sec, n_blk, n_chunk),
        out_shape=jax.ShapeDtypeStruct((TICKS, rows, nb * BLK), jnp.bfloat16),
        in_specs=[
            pl.BlockSpec(memory_space=pltpu.SMEM),
            pl.BlockSpec(memory_space=pltpu.VMEM),
            pl.BlockSpec(memory_space=pl.ANY),
            pl.BlockSpec(memory_space=pl.ANY),
        ],
        out_specs=pl.BlockSpec(memory_space=pltpu.VMEM),
        scratch_shapes=[
            pltpu.VMEM((nb, nz * BLK, BLK), jnp.bfloat16),
            pltpu.SemaphoreType.DMA((W_PIECES,)),
            pltpu.VMEM((nb, 1, BLK), jnp.float32),
            pltpu.VMEM((TICKS, nb, rows, BLK), jnp.bfloat16),
            pltpu.SemaphoreType.DMA((TICKS, n_chunk, 5)),
            pltpu.SemaphoreType.DMA((TICKS, n_chunk, 5)),
            pltpu.SemaphoreType.DMA((4,)),
        ] + [pltpu.VMEM((npad, rows // n_chunk, BLK), jnp.bfloat16) for _ in range(TICKS * n_chunk)],
        compiler_params=pltpu.CompilerParams(
            collective_id=0, has_side_effects=True, vmem_limit_bytes=VMEM_BYTES),
    )(source_block_indices[0].T, pend, w, bias)


def solution(mesh):
    n_sec = mesh.shape["section"]
    n_blk = mesh.shape["blk"]
    in_specs = (
        P("section", "blk"),
        P("section", "blk", None, None, None),
        P("section", "blk", None),
        P("section", "blk"),
    )
    out_specs = P(None, "section", "blk")
    return jax.shard_map(functools.partial(shards, n_sec, n_blk, ROW_CHUNKS), mesh=mesh, in_specs=in_specs,
                         out_specs=out_specs, check_vma=False)
```

```python
import functools

import jax
import jax.numpy as jnp
from jax import lax
from jax.experimental import pallas as pl
from jax.experimental.pallas import tpu as pltpu
from jax.sharding import PartitionSpec as P

BLK = 128
HALO = 4
TICKS = 8
ROW_CHUNKS = 2
W_PIECES = 4
VMEM_BYTES = 48 * 1024 * 1024
MESH = pl.DeviceIdType.MESH


def relay_kernel(n_sec, n_blk, n_chunk, src_ref, pend_ref, w_hbm, b_hbm, out_ref,
                 w_ref, w_sem, b_ref, sendbuf, send_sem, recv_sem, local_sem, *slot_list):
    n_piece = w_sem.shape[0]
    per_piece = w_hbm.shape[0] // n_piece
    w_copies = [pltpu.make_async_copy(w_hbm.at[pl.ds(j * per_piece, per_piece)],
                                      w_ref.at[pl.ds(j * per_piece, per_piece)], w_sem.at[j])
                for j in range(n_piece)]
    b_copy = pltpu.make_async_copy(b_hbm, b_ref, local_sem.at[3])
    b_copy.start()
    for cp in w_copies:
        cp.start()
    slots = [slot_list[t * n_chunk:(t + 1) * n_chunk] for t in range(TICKS)]
    s = lax.axis_index("section")
    d = lax.axis_index("blk")
    nb = pend_ref.shape[0]
    rc = pend_ref.shape[1] // n_chunk
    left = lax.rem(d + n_blk - 1, n_blk)
    right = lax.rem(d + 1, n_blk)
    s_next = jnp.minimum(s + 1, n_sec - 1)
    s_prev = jnp.maximum(s - 1, 0)

    n_cols = nb * n_blk
    col_shift = n_cols - d * nb + HALO
    n_pad = nb + 2 * HALO
    barrier = pltpu.get_barrier_semaphore()
    for nd in (left, right):
        pl.semaphore_signal(barrier, inc=1, device_id=(s, nd), device_id_type=MESH)

    @pl.when(s < n_sec - 1)
    def _():
        pl.semaphore_signal(barrier, inc=1, device_id=(s_next, d), device_id_type=MESH)

    @pl.when(s > 0)
    def _():
        pl.semaphore_signal(barrier, inc=1, device_id=(s_prev, d), device_id_type=MESH)

    has_prev = (s + n_sec - 1) // n_sec
    has_next = (2 * n_sec - 3 - s) // (n_sec - 1)
    pl.semaphore_wait(barrier, 2 + has_prev + has_next)

    def center_copies(t, c):
        rows = pl.ds(c * rc, rc)
        parts = ((3, 0, HALO), (4, nb - HALO, HALO), (0, HALO, nb - 2 * HALO))
        return [pltpu.make_async_remote_copy(
            src_ref=sendbuf.at[t - 1, pl.ds(lo, n), rows],
            dst_ref=slots[t][c].at[pl.ds(HALO + lo, n)],
            send_sem=send_sem.at[t, c, j], recv_sem=recv_sem.at[t, c, j],
            device_id=(s_next, d), device_id_type=MESH) for j, lo, n in parts]

    def edge_copies(src, t, c):
        lo = pltpu.make_async_remote_copy(
            src_ref=src.at[pl.ds(0, HALO)],
            dst_ref=slots[t][c].at[pl.ds(HALO + nb, HALO)],
            send_sem=send_sem.at[t, c, 1], recv_sem=recv_sem.at[t, c, 1],
            device_id=(s, left), device_id_type=MESH)
        hi = pltpu.make_async_remote_copy(
            src_ref=src.at[pl.ds(nb - HALO, HALO)],
            dst_ref=slots[t][c].at[pl.ds(0, HALO)],
            send_sem=send_sem.at[t, c, 2], recv_sem=recv_sem.at[t, c, 2],
            device_id=(s, right), device_id_type=MESH)
        return lo, hi

    first = [edge_copies(pend_ref.at[:, pl.ds(c * rc, rc)], 0, c) for c in range(n_chunk)]
    for pair in first:
        for cp in pair:
            cp.start()
    for c in range(n_chunk):
        own = pltpu.make_async_copy(pend_ref.at[:, pl.ds(c * rc, rc)], slots[0][c].at[pl.ds(HALO, nb)],
                                    local_sem.at[0])
        own.start()
        own.wait()
        for cp in first[c]:
            cp.wait_recv()

    def compute(t, c):
        work = slots[t][c]

        def row_body(i, carry):
            xs = [work[jnp.minimum(lax.rem(src_ref[k, i] + col_shift, n_cols), n_pad - 1)]
                  for k in range(w_ref.shape[1] // BLK)]
            xcat = jnp.concatenate(xs, axis=1)
            acc = jnp.dot(xcat, w_ref[i], preferred_element_type=jnp.float32)
            acc = acc + b_ref[i]
            y = jnp.maximum(acc, 0.0).astype(out_ref.dtype)
            sendbuf[t, i, pl.ds(c * rc, rc)] = y
            out_ref[t, pl.ds(c * rc, rc), pl.ds(pl.multiple_of(i * BLK, BLK), BLK)] = y
            return carry
        if t == 0 and c == 0:
            b_copy.wait()
            for j in range(n_piece):
                w_copies[j].wait()
                lax.fori_loop(j * per_piece, (j + 1) * per_piece, row_body, 0, unroll=8)
        else:
            lax.fori_loop(0, nb, row_body, 0, unroll=True)

    for t in range(TICKS):
        for c in range(n_chunk):
            if t > 0:
                @pl.when(s >= t)
                def _():
                    parts = center_copies(t, c)
                    parts[0].wait_recv()
                    parts[1].wait_recv()
                    fwd = edge_copies(slots[t][c].at[pl.ds(HALO, nb)], t, c)
                    for cp in fwd:
                        cp.start()
                    parts[2].wait_recv()
                    for cp in fwd:
                        cp.wait_recv()

            @pl.when(s >= t)
            def _():
                compute(t, c)

            @pl.when(s < t)
            def _():
                out_ref[t, pl.ds(c * rc, rc)] = jnp.zeros((rc, nb * BLK), out_ref.dtype)

            if t + 1 < TICKS:
                @pl.when((s >= t) & (s < n_sec - 1))
                def _():
                    for cp in center_copies(t + 1, c):
                        cp.start()

    for pair in first:
        for cp in pair:
            cp.wait_send()
    for t in range(TICKS - 1):
        @pl.when((s >= t) & (s < n_sec - 1))
        def _():
            for c in range(n_chunk):
                for cp in center_copies(t + 1, c):
                    cp.wait_send()
    for t in range(1, TICKS):
        @pl.when(s >= t)
        def _():
            for c in range(n_chunk):
                for cp in edge_copies(slots[t][c].at[pl.ds(HALO, nb)], t, c):
                    cp.wait_send()


def shards(n_sec, n_blk, n_chunk, pending_groups, coefficient_tiles, source_block_indices, additive_offsets):
    rows, units = pending_groups.shape
    nb = coefficient_tiles.shape[1]
    nz = coefficient_tiles.shape[2]
    pend = pending_groups.reshape(rows, nb, BLK).transpose(1, 0, 2)
    w = coefficient_tiles[0].reshape(nb, nz * BLK, BLK)
    bias = additive_offsets[0].reshape(nb, 1, BLK)
    npad = nb + 2 * HALO
    return pl.pallas_call(
        functools.partial(relay_kernel, n_sec, n_blk, n_chunk),
        out_shape=jax.ShapeDtypeStruct((TICKS, rows, nb * BLK), jnp.bfloat16),
        in_specs=[
            pl.BlockSpec(memory_space=pltpu.SMEM),
            pl.BlockSpec(memory_space=pltpu.VMEM),
            pl.BlockSpec(memory_space=pl.ANY),
            pl.BlockSpec(memory_space=pl.ANY),
        ],
        out_specs=pl.BlockSpec(memory_space=pltpu.VMEM),
        scratch_shapes=[
            pltpu.VMEM((nb, nz * BLK, BLK), jnp.bfloat16),
            pltpu.SemaphoreType.DMA((W_PIECES,)),
            pltpu.VMEM((nb, 1, BLK), jnp.float32),
            pltpu.VMEM((TICKS, nb, rows, BLK), jnp.bfloat16),
            pltpu.SemaphoreType.DMA((TICKS, n_chunk, 5)),
            pltpu.SemaphoreType.DMA((TICKS, n_chunk, 5)),
            pltpu.SemaphoreType.DMA((4,)),
        ] + [pltpu.VMEM((npad, rows // n_chunk, BLK), jnp.bfloat16) for _ in range(TICKS * n_chunk)],
        compiler_params=pltpu.CompilerParams(
            collective_id=0, has_side_effects=True, vmem_limit_bytes=VMEM_BYTES),
    )(source_block_indices[0].T, pend, w, bias)


def solution(mesh):
    n_sec = mesh.shape["section"]
    n_blk = mesh.shape["blk"]
    in_specs = (
        P("section", "blk"),
        P("section", "blk", None, None, None),
        P("section", "blk", None),
        P("section", "blk"),
    )
    out_specs = P(None, "section", "blk")
    return jax.shard_map(functools.partial(shards, n_sec, n_blk, ROW_CHUNKS), mesh=mesh, in_specs=in_specs,
                         out_specs=out_specs, check_vma=False)
```

```python
import functools

import jax
import jax.numpy as jnp
from jax import lax
from jax.experimental import pallas as pl
from jax.experimental.pallas import tpu as pltpu
from jax.sharding import PartitionSpec as P

BLK = 128
HALO = 4
TICKS = 8
ROW_CHUNKS = 2
W_PIECES = 4
VMEM_BYTES = 48 * 1024 * 1024
MESH = pl.DeviceIdType.MESH


def relay_kernel(n_sec, n_blk, n_chunk, src_ref, pend_ref, w_hbm, b_hbm, out_ref,
                 w_ref, w_sem, b_ref, sendbuf, send_sem, recv_sem, local_sem, *slot_list):
    n_piece = w_sem.shape[0]
    per_piece = w_hbm.shape[0] // n_piece
    w_copies = [pltpu.make_async_copy(w_hbm.at[pl.ds(j * per_piece, per_piece)],
                                      w_ref.at[pl.ds(j * per_piece, per_piece)], w_sem.at[j])
                for j in range(n_piece)]
    b_copy = pltpu.make_async_copy(b_hbm, b_ref, local_sem.at[3])
    b_copy.start()
    for cp in w_copies:
        cp.start()
    slots = [slot_list[t * n_chunk:(t + 1) * n_chunk] for t in range(TICKS)]
    s = lax.axis_index("section")
    d = lax.axis_index("blk")
    nb = pend_ref.shape[0]
    rc = pend_ref.shape[1] // n_chunk
    left = lax.rem(d + n_blk - 1, n_blk)
    right = lax.rem(d + 1, n_blk)
    s_next = jnp.minimum(s + 1, n_sec - 1)
    s_prev = jnp.maximum(s - 1, 0)

    n_cols = nb * n_blk
    col_shift = n_cols - d * nb + HALO
    n_pad = nb + 2 * HALO
    barrier = pltpu.get_barrier_semaphore()
    for nd in (left, right):
        pl.semaphore_signal(barrier, inc=1, device_id=(s, nd), device_id_type=MESH)

    @pl.when(s < n_sec - 1)
    def _():
        pl.semaphore_signal(barrier, inc=1, device_id=(s_next, d), device_id_type=MESH)

    @pl.when(s > 0)
    def _():
        pl.semaphore_signal(barrier, inc=1, device_id=(s_prev, d), device_id_type=MESH)

    has_prev = (s + n_sec - 1) // n_sec
    has_next = (2 * n_sec - 3 - s) // (n_sec - 1)
    pl.semaphore_wait(barrier, 2 + has_prev + has_next)

    def center_copies(t, c):
        rows = pl.ds(c * rc, rc)
        parts = ((3, 0, HALO), (4, nb - HALO, HALO), (0, HALO, nb - 2 * HALO))
        return [pltpu.make_async_remote_copy(
            src_ref=sendbuf.at[t - 1, pl.ds(lo, n), rows],
            dst_ref=slots[t][c].at[pl.ds(HALO + lo, n)],
            send_sem=send_sem.at[t, c, j], recv_sem=recv_sem.at[t, c, j],
            device_id=(s_next, d), device_id_type=MESH) for j, lo, n in parts]

    def edge_copies(src, t, c):
        lo = pltpu.make_async_remote_copy(
            src_ref=src.at[pl.ds(0, HALO)],
            dst_ref=slots[t][c].at[pl.ds(HALO + nb, HALO)],
            send_sem=send_sem.at[t, c, 1], recv_sem=recv_sem.at[t, c, 1],
            device_id=(s, left), device_id_type=MESH)
        hi = pltpu.make_async_remote_copy(
            src_ref=src.at[pl.ds(nb - HALO, HALO)],
            dst_ref=slots[t][c].at[pl.ds(0, HALO)],
            send_sem=send_sem.at[t, c, 2], recv_sem=recv_sem.at[t, c, 2],
            device_id=(s, right), device_id_type=MESH)
        return lo, hi

    first = [edge_copies(pend_ref.at[:, pl.ds(c * rc, rc)], 0, c) for c in range(n_chunk)]
    for pair in first:
        for cp in pair:
            cp.start()
    for c in range(n_chunk):
        own = pltpu.make_async_copy(pend_ref.at[:, pl.ds(c * rc, rc)], slots[0][c].at[pl.ds(HALO, nb)],
                                    local_sem.at[0])
        own.start()
        own.wait()
        for cp in first[c]:
            cp.wait_recv()

    def forward_edges(t, c):
        parts = center_copies(t, c)
        parts[0].wait_recv()
        parts[1].wait_recv()
        for cp in edge_copies(slots[t][c].at[pl.ds(HALO, nb)], t, c):
            cp.start()

    def compute(t, c, mid=None):
        work = slots[t][c]

        def row_body(i, carry):
            xs = [work[jnp.minimum(lax.rem(src_ref[k, i] + col_shift, n_cols), n_pad - 1)]
                  for k in range(w_ref.shape[1] // BLK)]
            xcat = jnp.concatenate(xs, axis=1)
            acc = jnp.dot(xcat, w_ref[i], preferred_element_type=jnp.float32)
            acc = acc + b_ref[i]
            y = jnp.maximum(acc, 0.0).astype(out_ref.dtype)
            sendbuf[t, i, pl.ds(c * rc, rc)] = y
            out_ref[t, pl.ds(c * rc, rc), pl.ds(pl.multiple_of(i * BLK, BLK), BLK)] = y
            return carry
        if t == 0 and c == 0:
            b_copy.wait()
            for j in range(n_piece):
                w_copies[j].wait()
                lax.fori_loop(j * per_piece, (j + 1) * per_piece, row_body, 0, unroll=8)
        elif mid is None:
            lax.fori_loop(0, nb, row_body, 0, unroll=True)
        else:
            lax.fori_loop(0, nb // 2, row_body, 0, unroll=True)
            mid()
            lax.fori_loop(nb // 2, nb, row_body, 0, unroll=True)

    for t in range(TICKS):
        for c in range(n_chunk):
            if t > 0:
                @pl.when(s >= t)
                def _():
                    parts = center_copies(t, c)
                    fwd = edge_copies(slots[t][c].at[pl.ds(HALO, nb)], t, c)
                    if c == 0:
                        forward_edges(t, c)
                    parts[2].wait_recv()
                    for cp in fwd:
                        cp.wait_recv()

            @pl.when(s >= t)
            def _():
                if t > 0 and c + 1 < n_chunk:
                    compute(t, c, functools.partial(forward_edges, t, c + 1))
                else:
                    compute(t, c)

            @pl.when(s < t)
            def _():
                out_ref[t, pl.ds(c * rc, rc)] = jnp.zeros((rc, nb * BLK), out_ref.dtype)

            if t + 1 < TICKS:
                @pl.when((s >= t) & (s < n_sec - 1))
                def _():
                    for cp in center_copies(t + 1, c):
                        cp.start()

    for pair in first:
        for cp in pair:
            cp.wait_send()
    for t in range(TICKS - 1):
        @pl.when((s >= t) & (s < n_sec - 1))
        def _():
            for c in range(n_chunk):
                for cp in center_copies(t + 1, c):
                    cp.wait_send()
    for t in range(1, TICKS):
        @pl.when(s >= t)
        def _():
            for c in range(n_chunk):
                for cp in edge_copies(slots[t][c].at[pl.ds(HALO, nb)], t, c):
                    cp.wait_send()


def shards(n_sec, n_blk, n_chunk, pending_groups, coefficient_tiles, source_block_indices, additive_offsets):
    rows, units = pending_groups.shape
    nb = coefficient_tiles.shape[1]
    nz = coefficient_tiles.shape[2]
    pend = pending_groups.reshape(rows, nb, BLK).transpose(1, 0, 2)
    w = coefficient_tiles[0].reshape(nb, nz * BLK, BLK)
    bias = additive_offsets[0].reshape(nb, 1, BLK)
    npad = nb + 2 * HALO
    return pl.pallas_call(
        functools.partial(relay_kernel, n_sec, n_blk, n_chunk),
        out_shape=jax.ShapeDtypeStruct((TICKS, rows, nb * BLK), jnp.bfloat16),
        in_specs=[
            pl.BlockSpec(memory_space=pltpu.SMEM),
            pl.BlockSpec(memory_space=pltpu.VMEM),
            pl.BlockSpec(memory_space=pl.ANY),
            pl.BlockSpec(memory_space=pl.ANY),
        ],
        out_specs=pl.BlockSpec(memory_space=pltpu.VMEM),
        scratch_shapes=[
            pltpu.VMEM((nb, nz * BLK, BLK), jnp.bfloat16),
            pltpu.SemaphoreType.DMA((W_PIECES,)),
            pltpu.VMEM((nb, 1, BLK), jnp.float32),
            pltpu.VMEM((TICKS, nb, rows, BLK), jnp.bfloat16),
            pltpu.SemaphoreType.DMA((TICKS, n_chunk, 5)),
            pltpu.SemaphoreType.DMA((TICKS, n_chunk, 5)),
            pltpu.SemaphoreType.DMA((4,)),
        ] + [pltpu.VMEM((npad, rows // n_chunk, BLK), jnp.bfloat16) for _ in range(TICKS * n_chunk)],
        compiler_params=pltpu.CompilerParams(
            collective_id=0, has_side_effects=True, vmem_limit_bytes=VMEM_BYTES),
    )(source_block_indices[0].T, pend, w, bias)


def solution(mesh):
    n_sec = mesh.shape["section"]
    n_blk = mesh.shape["blk"]
    in_specs = (
        P("section", "blk"),
        P("section", "blk", None, None, None),
        P("section", "blk", None),
        P("section", "blk"),
    )
    out_specs = P(None, "section", "blk")
    return jax.shard_map(functools.partial(shards, n_sec, n_blk, ROW_CHUNKS), mesh=mesh, in_specs=in_specs,
                         out_specs=out_specs, check_vma=False)
```

```python
import functools

import jax
import jax.numpy as jnp
from jax import lax
from jax.experimental import pallas as pl
from jax.experimental.pallas import tpu as pltpu
from jax.sharding import PartitionSpec as P

BLK = 128
HALO = 4
TICKS = 8
ROW_CHUNKS = 2
W_PIECES = 8
VMEM_BYTES = 48 * 1024 * 1024
MESH = pl.DeviceIdType.MESH


def relay_kernel(n_sec, n_blk, n_chunk, src_ref, pend_ref, w_hbm, b_hbm, out_ref,
                 w_ref, w_sem, b_ref, sendbuf, send_sem, recv_sem, local_sem, *slot_list):
    n_piece = w_sem.shape[0]
    per_piece = w_hbm.shape[0] // n_piece
    w_copies = [pltpu.make_async_copy(w_hbm.at[pl.ds(j * per_piece, per_piece)],
                                      w_ref.at[pl.ds(j * per_piece, per_piece)], w_sem.at[j])
                for j in range(n_piece)]
    b_copy = pltpu.make_async_copy(b_hbm, b_ref, local_sem.at[3])
    b_copy.start()
    for cp in w_copies:
        cp.start()
    slots = [slot_list[t * n_chunk:(t + 1) * n_chunk] for t in range(TICKS)]
    rc0 = pend_ref.shape[1] // n_chunk
    nb0 = pend_ref.shape[0]
    own = [pltpu.make_async_copy(pend_ref.at[:, pl.ds(c * rc0, rc0)], slots[0][c].at[pl.ds(HALO, nb0)],
                                 local_sem.at[c]) for c in range(n_chunk)]
    for cp in own:
        cp.start()
    s = lax.axis_index("section")
    d = lax.axis_index("blk")
    nb = pend_ref.shape[0]
    rc = pend_ref.shape[1] // n_chunk
    left = lax.rem(d + n_blk - 1, n_blk)
    right = lax.rem(d + 1, n_blk)
    s_next = jnp.minimum(s + 1, n_sec - 1)
    s_prev = jnp.maximum(s - 1, 0)

    n_cols = nb * n_blk
    col_shift = n_cols - d * nb + HALO
    n_pad = nb + 2 * HALO
    barrier = pltpu.get_barrier_semaphore()
    for nd in (left, right):
        pl.semaphore_signal(barrier, inc=1, device_id=(s, nd), device_id_type=MESH)

    @pl.when(s < n_sec - 1)
    def _():
        pl.semaphore_signal(barrier, inc=1, device_id=(s_next, d), device_id_type=MESH)

    @pl.when(s > 0)
    def _():
        pl.semaphore_signal(barrier, inc=1, device_id=(s_prev, d), device_id_type=MESH)

    has_prev = (s + n_sec - 1) // n_sec
    has_next = (2 * n_sec - 3 - s) // (n_sec - 1)
    pl.semaphore_wait(barrier, 2 + has_prev + has_next)

    def center_copies(t, c):
        rows = pl.ds(c * rc, rc)
        parts = ((3, 0, HALO), (4, nb - HALO, HALO), (0, HALO, nb - 2 * HALO))
        return [pltpu.make_async_remote_copy(
            src_ref=sendbuf.at[t - 1, pl.ds(lo, n), rows],
            dst_ref=slots[t][c].at[pl.ds(HALO + lo, n)],
            send_sem=send_sem.at[t, c, j], recv_sem=recv_sem.at[t, c, j],
            device_id=(s_next, d), device_id_type=MESH) for j, lo, n in parts]

    def edge_copies(src, t, c):
        lo = pltpu.make_async_remote_copy(
            src_ref=src.at[pl.ds(0, HALO)],
            dst_ref=slots[t][c].at[pl.ds(HALO + nb, HALO)],
            send_sem=send_sem.at[t, c, 1], recv_sem=recv_sem.at[t, c, 1],
            device_id=(s, left), device_id_type=MESH)
        hi = pltpu.make_async_remote_copy(
            src_ref=src.at[pl.ds(nb - HALO, HALO)],
            dst_ref=slots[t][c].at[pl.ds(0, HALO)],
            send_sem=send_sem.at[t, c, 2], recv_sem=recv_sem.at[t, c, 2],
            device_id=(s, right), device_id_type=MESH)
        return lo, hi

    first = [edge_copies(pend_ref.at[:, pl.ds(c * rc, rc)], 0, c) for c in range(n_chunk)]
    for pair in first:
        for cp in pair:
            cp.start()

    def compute(t, c):
        work = slots[t][c]

        def row_body(i, carry):
            xs = [work[jnp.minimum(lax.rem(src_ref[k, i] + col_shift, n_cols), n_pad - 1)]
                  for k in range(w_ref.shape[1] // BLK)]
            xcat = jnp.concatenate(xs, axis=1)
            acc = jnp.dot(xcat, w_ref[i], preferred_element_type=jnp.float32)
            acc = acc + b_ref[i]
            y = jnp.maximum(acc, 0.0).astype(out_ref.dtype)
            sendbuf[t, i, pl.ds(c * rc, rc)] = y
            out_ref[t, pl.ds(c * rc, rc), pl.ds(pl.multiple_of(i * BLK, BLK), BLK)] = y
            return carry
        if t == 0 and c == 0:
            b_copy.wait()
            for j in range(n_piece):
                w_copies[j].wait()
                lax.fori_loop(j * per_piece, (j + 1) * per_piece, row_body, 0, unroll=8)
        else:
            lax.fori_loop(0, nb, row_body, 0, unroll=True)

    for t in range(TICKS):
        for c in range(n_chunk):
            if t == 0:
                own[c].wait()
                for cp in first[c]:
                    cp.wait_recv()
            if t > 0:
                @pl.when(s >= t)
                def _():
                    parts = center_copies(t, c)
                    parts[0].wait_recv()
                    parts[1].wait_recv()
                    fwd = edge_copies(slots[t][c].at[pl.ds(HALO, nb)], t, c)
                    for cp in fwd:
                        cp.start()
                    parts[2].wait_recv()
                    for cp in fwd:
                        cp.wait_recv()

            @pl.when(s >= t)
            def _():
                compute(t, c)

            @pl.when(s < t)
            def _():
                out_ref[t, pl.ds(c * rc, rc)] = jnp.zeros((rc, nb * BLK), out_ref.dtype)

            if t + 1 < TICKS:
                @pl.when((s >= t) & (s < n_sec - 1))
                def _():
                    for cp in center_copies(t + 1, c):
                        cp.start()

    for pair in first:
        for cp in pair:
            cp.wait_send()
    for t in range(TICKS - 1):
        @pl.when((s >= t) & (s < n_sec - 1))
        def _():
            for c in range(n_chunk):
                for cp in center_copies(t + 1, c):
                    cp.wait_send()
    for t in range(1, TICKS):
        @pl.when(s >= t)
        def _():
            for c in range(n_chunk):
                for cp in edge_copies(slots[t][c].at[pl.ds(HALO, nb)], t, c):
                    cp.wait_send()


def shards(n_sec, n_blk, n_chunk, pending_groups, coefficient_tiles, source_block_indices, additive_offsets):
    rows, units = pending_groups.shape
    nb = coefficient_tiles.shape[1]
    nz = coefficient_tiles.shape[2]
    pend = pending_groups.reshape(rows, nb, BLK).transpose(1, 0, 2)
    w = coefficient_tiles[0].reshape(nb, nz * BLK, BLK)
    bias = additive_offsets[0].reshape(nb, 1, BLK)
    npad = nb + 2 * HALO
    return pl.pallas_call(
        functools.partial(relay_kernel, n_sec, n_blk, n_chunk),
        out_shape=jax.ShapeDtypeStruct((TICKS, rows, nb * BLK), jnp.bfloat16),
        in_specs=[
            pl.BlockSpec(memory_space=pltpu.SMEM),
            pl.BlockSpec(memory_space=pltpu.VMEM),
            pl.BlockSpec(memory_space=pl.ANY),
            pl.BlockSpec(memory_space=pl.ANY),
        ],
        out_specs=pl.BlockSpec(memory_space=pltpu.VMEM),
        scratch_shapes=[
            pltpu.VMEM((nb, nz * BLK, BLK), jnp.bfloat16),
            pltpu.SemaphoreType.DMA((W_PIECES,)),
            pltpu.VMEM((nb, 1, BLK), jnp.float32),
            pltpu.VMEM((TICKS, nb, rows, BLK), jnp.bfloat16),
            pltpu.SemaphoreType.DMA((TICKS, n_chunk, 5)),
            pltpu.SemaphoreType.DMA((TICKS, n_chunk, 5)),
            pltpu.SemaphoreType.DMA((4,)),
        ] + [pltpu.VMEM((npad, rows // n_chunk, BLK), jnp.bfloat16) for _ in range(TICKS * n_chunk)],
        compiler_params=pltpu.CompilerParams(
            collective_id=0, has_side_effects=True, vmem_limit_bytes=VMEM_BYTES),
    )(source_block_indices[0].T, pend, w, bias)


def solution(mesh):
    n_sec = mesh.shape["section"]
    n_blk = mesh.shape["blk"]
    in_specs = (
        P("section", "blk"),
        P("section", "blk", None, None, None),
        P("section", "blk", None),
        P("section", "blk"),
    )
    out_specs = P(None, "section", "blk")
    return jax.shard_map(functools.partial(shards, n_sec, n_blk, ROW_CHUNKS), mesh=mesh, in_specs=in_specs,
                         out_specs=out_specs, check_vma=False)
```

```python
import functools

import jax
import jax.numpy as jnp
from jax import lax
from jax.experimental import pallas as pl
from jax.experimental.pallas import tpu as pltpu
from jax.sharding import PartitionSpec as P

BLK = 128
HALO = 4
TICKS = 8
ROW_CHUNKS = 2
W_PIECES = 2
VMEM_BYTES = 48 * 1024 * 1024
MESH = pl.DeviceIdType.MESH


def relay_kernel(n_sec, n_blk, n_chunk, src_ref, pend_ref, w_hbm, b_hbm, out_ref,
                 w_ref, w_sem, b_ref, sendbuf, send_sem, recv_sem, local_sem, *slot_list):
    n_piece = w_sem.shape[0]
    per_piece = w_hbm.shape[0] // n_piece
    w_copies = [pltpu.make_async_copy(w_hbm.at[pl.ds(j * per_piece, per_piece)],
                                      w_ref.at[pl.ds(j * per_piece, per_piece)], w_sem.at[j])
                for j in range(n_piece)]
    b_copy = pltpu.make_async_copy(b_hbm, b_ref, local_sem.at[3])
    b_copy.start()
    for cp in w_copies:
        cp.start()
    slots = [slot_list[t * n_chunk:(t + 1) * n_chunk] for t in range(TICKS)]
    s = lax.axis_index("section")
    d = lax.axis_index("blk")
    nb = pend_ref.shape[0]
    rc = pend_ref.shape[1] // n_chunk
    left = lax.rem(d + n_blk - 1, n_blk)
    right = lax.rem(d + 1, n_blk)
    s_next = jnp.minimum(s + 1, n_sec - 1)
    s_prev = jnp.maximum(s - 1, 0)

    n_cols = nb * n_blk
    col_shift = n_cols - d * nb + HALO
    n_pad = nb + 2 * HALO
    barrier = pltpu.get_barrier_semaphore()
    for nd in (left, right):
        pl.semaphore_signal(barrier, inc=1, device_id=(s, nd), device_id_type=MESH)

    @pl.when(s < n_sec - 1)
    def _():
        pl.semaphore_signal(barrier, inc=1, device_id=(s_next, d), device_id_type=MESH)

    @pl.when(s > 0)
    def _():
        pl.semaphore_signal(barrier, inc=1, device_id=(s_prev, d), device_id_type=MESH)

    has_prev = (s + n_sec - 1) // n_sec
    has_next = (2 * n_sec - 3 - s) // (n_sec - 1)
    pl.semaphore_wait(barrier, 2 + has_prev + has_next)

    def center_copies(t, c):
        rows = pl.ds(c * rc, rc)
        parts = ((3, 0, HALO), (4, nb - HALO, HALO), (0, HALO, nb - 2 * HALO))
        return [pltpu.make_async_remote_copy(
            src_ref=sendbuf.at[t - 1, pl.ds(lo, n), rows],
            dst_ref=slots[t][c].at[pl.ds(HALO + lo, n)],
            send_sem=send_sem.at[t, c, j], recv_sem=recv_sem.at[t, c, j],
            device_id=(s_next, d), device_id_type=MESH) for j, lo, n in parts]

    def edge_copies(src, t, c):
        lo = pltpu.make_async_remote_copy(
            src_ref=src.at[pl.ds(0, HALO)],
            dst_ref=slots[t][c].at[pl.ds(HALO + nb, HALO)],
            send_sem=send_sem.at[t, c, 1], recv_sem=recv_sem.at[t, c, 1],
            device_id=(s, left), device_id_type=MESH)
        hi = pltpu.make_async_remote_copy(
            src_ref=src.at[pl.ds(nb - HALO, HALO)],
            dst_ref=slots[t][c].at[pl.ds(0, HALO)],
            send_sem=send_sem.at[t, c, 2], recv_sem=recv_sem.at[t, c, 2],
            device_id=(s, right), device_id_type=MESH)
        return lo, hi

    first = [edge_copies(pend_ref.at[:, pl.ds(c * rc, rc)], 0, c) for c in range(n_chunk)]
    for pair in first:
        for cp in pair:
            cp.start()
    for c in range(n_chunk):
        own = pltpu.make_async_copy(pend_ref.at[:, pl.ds(c * rc, rc)], slots[0][c].at[pl.ds(HALO, nb)],
                                    local_sem.at[0])
        own.start()
        own.wait()
        for cp in first[c]:
            cp.wait_recv()

    def compute(t, c):
        work = slots[t][c]

        def row_body(i, carry):
            xs = [work[jnp.minimum(lax.rem(src_ref[k, i] + col_shift, n_cols), n_pad - 1)]
                  for k in range(w_ref.shape[1] // BLK)]
            xcat = jnp.concatenate(xs, axis=1)
            acc = jnp.dot(xcat, w_ref[i], preferred_element_type=jnp.float32)
            acc = acc + b_ref[i]
            y = jnp.maximum(acc, 0.0).astype(out_ref.dtype)
            sendbuf[t, i, pl.ds(c * rc, rc)] = y
            out_ref[t, pl.ds(c * rc, rc), pl.ds(pl.multiple_of(i * BLK, BLK), BLK)] = y
            return carry
        if t == 0 and c == 0:
            b_copy.wait()
            for j in range(n_piece):
                w_copies[j].wait()
                lax.fori_loop(j * per_piece, (j + 1) * per_piece, row_body, 0, unroll=8)
        else:
            lax.fori_loop(0, nb, row_body, 0, unroll=True)

    for t in range(TICKS):
        for c in range(n_chunk):
            if t > 0:
                @pl.when(s >= t)
                def _():
                    parts = center_copies(t, c)
                    parts[0].wait_recv()
                    parts[1].wait_recv()
                    fwd = edge_copies(slots[t][c].at[pl.ds(HALO, nb)], t, c)
                    for cp in fwd:
                        cp.start()
                    parts[2].wait_recv()
                    for cp in fwd:
                        cp.wait_recv()

            @pl.when(s >= t)
            def _():
                compute(t, c)

            @pl.when(s < t)
            def _():
                out_ref[t, pl.ds(c * rc, rc)] = jnp.zeros((rc, nb * BLK), out_ref.dtype)

            if t + 1 < TICKS:
                @pl.when((s >= t) & (s < n_sec - 1))
                def _():
                    for cp in center_copies(t + 1, c):
                        cp.start()

    for pair in first:
        for cp in pair:
            cp.wait_send()
    for t in range(TICKS - 1):
        @pl.when((s >= t) & (s < n_sec - 1))
        def _():
            for c in range(n_chunk):
                for cp in center_copies(t + 1, c):
                    cp.wait_send()
    for t in range(1, TICKS):
        @pl.when(s >= t)
        def _():
            for c in range(n_chunk):
                for cp in edge_copies(slots[t][c].at[pl.ds(HALO, nb)], t, c):
                    cp.wait_send()


def shards(n_sec, n_blk, n_chunk, pending_groups, coefficient_tiles, source_block_indices, additive_offsets):
    rows, units = pending_groups.shape
    nb = coefficient_tiles.shape[1]
    nz = coefficient_tiles.shape[2]
    pend = pending_groups.reshape(rows, nb, BLK).transpose(1, 0, 2)
    w = coefficient_tiles[0].reshape(nb, nz * BLK, BLK)
    bias = additive_offsets[0].reshape(nb, 1, BLK)
    npad = nb + 2 * HALO
    return pl.pallas_call(
        functools.partial(relay_kernel, n_sec, n_blk, n_chunk),
        out_shape=jax.ShapeDtypeStruct((TICKS, rows, nb * BLK), jnp.bfloat16),
        in_specs=[
            pl.BlockSpec(memory_space=pltpu.SMEM),
            pl.BlockSpec(memory_space=pltpu.VMEM),
            pl.BlockSpec(memory_space=pl.ANY),
            pl.BlockSpec(memory_space=pl.ANY),
        ],
        out_specs=pl.BlockSpec(memory_space=pltpu.VMEM),
        scratch_shapes=[
            pltpu.VMEM((nb, nz * BLK, BLK), jnp.bfloat16),
            pltpu.SemaphoreType.DMA((W_PIECES,)),
            pltpu.VMEM((nb, 1, BLK), jnp.float32),
            pltpu.VMEM((TICKS, nb, rows, BLK), jnp.bfloat16),
            pltpu.SemaphoreType.DMA((TICKS, n_chunk, 5)),
            pltpu.SemaphoreType.DMA((TICKS, n_chunk, 5)),
            pltpu.SemaphoreType.DMA((4,)),
        ] + [pltpu.VMEM((npad, rows // n_chunk, BLK), jnp.bfloat16) for _ in range(TICKS * n_chunk)],
        compiler_params=pltpu.CompilerParams(
            collective_id=0, has_side_effects=True, vmem_limit_bytes=VMEM_BYTES),
    )(source_block_indices[0].T, pend, w, bias)


def solution(mesh):
    n_sec = mesh.shape["section"]
    n_blk = mesh.shape["blk"]
    in_specs = (
        P("section", "blk"),
        P("section", "blk", None, None, None),
        P("section", "blk", None),
        P("section", "blk"),
    )
    out_specs = P(None, "section", "blk")
    return jax.shard_map(functools.partial(shards, n_sec, n_blk, ROW_CHUNKS), mesh=mesh, in_specs=in_specs,
                         out_specs=out_specs, check_vma=False)
```

```python
import functools

import jax
import jax.numpy as jnp
from jax import lax
from jax.experimental import pallas as pl
from jax.experimental.pallas import tpu as pltpu
from jax.sharding import PartitionSpec as P

BLK = 128
HALO = 4
TICKS = 8
ROW_CHUNKS = 2
W_PIECES = 2
VMEM_BYTES = 48 * 1024 * 1024
MESH = pl.DeviceIdType.MESH


def relay_kernel(n_sec, n_blk, n_chunk, src_ref, pend_ref, w_hbm, b_hbm, out_ref,
                 w_ref, w_sem, b_ref, sendbuf, send_sem, recv_sem, local_sem, *slot_list):
    n_piece = w_sem.shape[0]
    per_piece = w_hbm.shape[0] // n_piece
    w_copies = [pltpu.make_async_copy(w_hbm.at[pl.ds(j * per_piece, per_piece)],
                                      w_ref.at[pl.ds(j * per_piece, per_piece)], w_sem.at[j])
                for j in range(n_piece)]
    b_copy = pltpu.make_async_copy(b_hbm, b_ref, local_sem.at[3])
    b_copy.start()
    for cp in w_copies:
        cp.start()
    slots = [slot_list[t * n_chunk:(t + 1) * n_chunk] for t in range(TICKS)]
    s = lax.axis_index("section")
    d = lax.axis_index("blk")
    nb = pend_ref.shape[0]
    rc = pend_ref.shape[1] // n_chunk
    left = lax.rem(d + n_blk - 1, n_blk)
    right = lax.rem(d + 1, n_blk)
    s_next = jnp.minimum(s + 1, n_sec - 1)
    s_prev = jnp.maximum(s - 1, 0)

    n_cols = nb * n_blk
    col_shift = n_cols - d * nb + HALO
    n_pad = nb + 2 * HALO
    barrier = pltpu.get_barrier_semaphore()
    for nd in (left, right):
        pl.semaphore_signal(barrier, inc=1, device_id=(s, nd), device_id_type=MESH)

    @pl.when(s < n_sec - 1)
    def _():
        pl.semaphore_signal(barrier, inc=1, device_id=(s_next, d), device_id_type=MESH)

    @pl.when(s > 0)
    def _():
        pl.semaphore_signal(barrier, inc=1, device_id=(s_prev, d), device_id_type=MESH)

    has_prev = (s + n_sec - 1) // n_sec
    has_next = (2 * n_sec - 3 - s) // (n_sec - 1)
    pl.semaphore_wait(barrier, 2 + has_prev + has_next)

    def center_copies(t, c):
        rows = pl.ds(c * rc, rc)
        parts = ((3, 0, HALO), (4, nb - HALO, HALO), (0, HALO, nb - 2 * HALO))
        return [pltpu.make_async_remote_copy(
            src_ref=sendbuf.at[t - 1, pl.ds(lo, n), rows],
            dst_ref=slots[t][c].at[pl.ds(HALO + lo, n)],
            send_sem=send_sem.at[t, c, j], recv_sem=recv_sem.at[t, c, j],
            device_id=(s_next, d), device_id_type=MESH) for j, lo, n in parts]

    def edge_copies(src, t, c):
        lo = pltpu.make_async_remote_copy(
            src_ref=src.at[pl.ds(0, HALO)],
            dst_ref=slots[t][c].at[pl.ds(HALO + nb, HALO)],
            send_sem=send_sem.at[t, c, 1], recv_sem=recv_sem.at[t, c, 1],
            device_id=(s, left), device_id_type=MESH)
        hi = pltpu.make_async_remote_copy(
            src_ref=src.at[pl.ds(nb - HALO, HALO)],
            dst_ref=slots[t][c].at[pl.ds(0, HALO)],
            send_sem=send_sem.at[t, c, 2], recv_sem=recv_sem.at[t, c, 2],
            device_id=(s, right), device_id_type=MESH)
        return lo, hi

    first = [edge_copies(pend_ref.at[:, pl.ds(c * rc, rc)], 0, c) for c in range(n_chunk)]
    for pair in first:
        for cp in pair:
            cp.start()
    for c in range(n_chunk):
        own = pltpu.make_async_copy(pend_ref.at[:, pl.ds(c * rc, rc)], slots[0][c].at[pl.ds(HALO, nb)],
                                    local_sem.at[0])
        own.start()
        own.wait()
        for cp in first[c]:
            cp.wait_recv()

    def compute(t, c):
        work = slots[t][c]

        def row_body(i, carry):
            xs = [work[jnp.minimum(lax.rem(src_ref[k, i] + col_shift, n_cols), n_pad - 1)]
                  for k in range(w_ref.shape[1] // BLK)]
            xcat = jnp.concatenate(xs, axis=1)
            acc = jnp.dot(xcat, w_ref[i], preferred_element_type=jnp.float32)
            acc = acc + b_ref[i]
            y = jnp.maximum(acc, 0.0).astype(out_ref.dtype)
            sendbuf[t, i, pl.ds(c * rc, rc)] = y
            out_ref[t, pl.ds(c * rc, rc), pl.ds(pl.multiple_of(i * BLK, BLK), BLK)] = y
            return carry
        if t == 0 and c == 0:
            b_copy.wait()
            for j in range(n_piece):
                w_copies[j].wait()
                lax.fori_loop(j * per_piece, (j + 1) * per_piece, row_body, 0, unroll=True)
        else:
            lax.fori_loop(0, nb, row_body, 0, unroll=True)

    for t in range(TICKS):
        for c in range(n_chunk):
            if t > 0:
                @pl.when(s >= t)
                def _():
                    parts = center_copies(t, c)
                    parts[0].wait_recv()
                    parts[1].wait_recv()
                    fwd = edge_copies(slots[t][c].at[pl.ds(HALO, nb)], t, c)
                    for cp in fwd:
                        cp.start()
                    parts[2].wait_recv()
                    for cp in fwd:
                        cp.wait_recv()

            @pl.when(s >= t)
            def _():
                compute(t, c)

            @pl.when(s < t)
            def _():
                out_ref[t, pl.ds(c * rc, rc)] = jnp.zeros((rc, nb * BLK), out_ref.dtype)

            if t + 1 < TICKS:
                @pl.when((s >= t) & (s < n_sec - 1))
                def _():
                    for cp in center_copies(t + 1, c):
                        cp.start()

    for pair in first:
        for cp in pair:
            cp.wait_send()
    for t in range(TICKS - 1):
        @pl.when((s >= t) & (s < n_sec - 1))
        def _():
            for c in range(n_chunk):
                for cp in center_copies(t + 1, c):
                    cp.wait_send()
    for t in range(1, TICKS):
        @pl.when(s >= t)
        def _():
            for c in range(n_chunk):
                for cp in edge_copies(slots[t][c].at[pl.ds(HALO, nb)], t, c):
                    cp.wait_send()


def shards(n_sec, n_blk, n_chunk, pending_groups, coefficient_tiles, source_block_indices, additive_offsets):
    rows, units = pending_groups.shape
    nb = coefficient_tiles.shape[1]
    nz = coefficient_tiles.shape[2]
    pend = pending_groups.reshape(rows, nb, BLK).transpose(1, 0, 2)
    w = coefficient_tiles[0].reshape(nb, nz * BLK, BLK)
    bias = additive_offsets[0].reshape(nb, 1, BLK)
    npad = nb + 2 * HALO
    return pl.pallas_call(
        functools.partial(relay_kernel, n_sec, n_blk, n_chunk),
        out_shape=jax.ShapeDtypeStruct((TICKS, rows, nb * BLK), jnp.bfloat16),
        in_specs=[
            pl.BlockSpec(memory_space=pltpu.SMEM),
            pl.BlockSpec(memory_space=pltpu.VMEM),
            pl.BlockSpec(memory_space=pl.ANY),
            pl.BlockSpec(memory_space=pl.ANY),
        ],
        out_specs=pl.BlockSpec(memory_space=pltpu.VMEM),
        scratch_shapes=[
            pltpu.VMEM((nb, nz * BLK, BLK), jnp.bfloat16),
            pltpu.SemaphoreType.DMA((W_PIECES,)),
            pltpu.VMEM((nb, 1, BLK), jnp.float32),
            pltpu.VMEM((TICKS, nb, rows, BLK), jnp.bfloat16),
            pltpu.SemaphoreType.DMA((TICKS, n_chunk, 5)),
            pltpu.SemaphoreType.DMA((TICKS, n_chunk, 5)),
            pltpu.SemaphoreType.DMA((4,)),
        ] + [pltpu.VMEM((npad, rows // n_chunk, BLK), jnp.bfloat16) for _ in range(TICKS * n_chunk)],
        compiler_params=pltpu.CompilerParams(
            collective_id=0, has_side_effects=True, vmem_limit_bytes=VMEM_BYTES),
    )(source_block_indices[0].T, pend, w, bias)


def solution(mesh):
    n_sec = mesh.shape["section"]
    n_blk = mesh.shape["blk"]
    in_specs = (
        P("section", "blk"),
        P("section", "blk", None, None, None),
        P("section", "blk", None),
        P("section", "blk"),
    )
    out_specs = P(None, "section", "blk")
    return jax.shard_map(functools.partial(shards, n_sec, n_blk, ROW_CHUNKS), mesh=mesh, in_specs=in_specs,
                         out_specs=out_specs, check_vma=False)
```
